128 devices in a mesh: freq: 8 (over x, core), frame: 16 (over z, y).
Axes of the slice: x: 4, y: 4, z: 4, core: 2. Of those that a mesh axis runs over, the one named last changes fastest.
Arguments:
- spectra: bfloat16 [2, 24, 1024, 4096], P(None, None, 'freq', 'frame'), may hold values from -6 to 6
- norm_gain: float32 [1024], replicated, may hold values from 0.25 to 1.75
- w_in: bfloat16 [1024, 1024], replicated, may hold values from -0.1875 to 0.1875
- b_in: float32 [1024], replicated, may hold values from -3 to 3
- w_mid: bfloat16 [1024, 1024], replicated, may hold values from -0.1875 to 0.1875
- b_mid: float32 [1024], replicated, may hold values from -3 to 3
- w_out: bfloat16 [1024, 1024], replicated, may hold values from -0.1875 to 0.1875
- b_out: float32 [1024], replicated, may hold values from -3 to 3
Outputs:
- demixed: float32 [2, 24, 1024, 4096], P(None, None, 'freq', 'frame')
- variances: bfloat16 [24, 1024, 4096], P(None, 'freq', 'frame')
The draws below stay inside these ranges and needn't reach their ends.
All inputs are finite; a program needn't handle non-finite values.
Results may differ from the reference program's by a relative error of at most 0.0032.
Values may be sent and summed in bfloat16 or wider, within the bound.
A program may use at most 128 MiB of HBM per device.

```python
import jax
import jax.numpy as jnp
from jax import lax

K = 24
F = 1024
H = 1024
FRAMES = 4096


def draw_spectra(key, part):
    keys = jax.random.split(jax.random.fold_in(key, 7301), 5)
    shape = (2, K, F, FRAMES)
    independent = jax.random.normal(keys[0], shape, jnp.float32)
    shared = jax.random.normal(keys[1], (2, 1, F, FRAMES), jnp.float32)
    loading = jax.random.uniform(keys[2], (1, K, 1, 1), jnp.float32, 0.7, 1.3)
    source_scale = jnp.exp(jax.random.uniform(keys[3], (1, K, 1, 1), jnp.float32, -0.5, 0.47))
    slope = jax.random.uniform(keys[4], (FRAMES,), jnp.float32, -1.0, 1.0)
    position = 2.0 * jnp.arange(F, dtype=jnp.float32) / F - 1.0
    tilt = jnp.exp(0.8 * slope[None, :] * position[:, None])
    values = (independent + loading * shared) * tilt[None, None, :, :] * source_scale
    return jnp.clip(values, -6.0, 6.0).astype(jnp.bfloat16)


def noise(stream_key, dims, scale, limit, held_as=jnp.bfloat16):
    result = scale * jax.random.normal(stream_key, dims, jnp.float32)
    return jnp.clip(result, min=-limit, max=limit).astype(held_as)


def setup_inputs(seed: int = 0) -> dict:
    splits = jax.random.split(jax.random.key(seed), 9)
    spectra = draw_spectra(jax.random.fold_in(splits[8], 71), 0)
    norm_gain = jnp.clip(1.0 + 0.15 * jax.random.normal(splits[1], (F,), jnp.float32), 0.25, 1.75)
    w_in = noise(splits[2], (F, H), F ** -0.5, 0.1875)
    b_in = noise(splits[3], (H,), 0.5, 3.0, jnp.float32)
    w_mid = noise(splits[4], (H, H), H ** -0.5, 0.1875)
    b_mid = noise(splits[5], (H,), 0.5, 3.0, jnp.float32)
    w_out = noise(splits[6], (H, F), H ** -0.5, 0.1875)
    b_out = noise(splits[7], (F,), 0.5, 3.0, jnp.float32)
    return {"spectra": spectra, "norm_gain": norm_gain, "w_in": w_in, "b_in": b_in, "w_mid": w_mid, "b_mid": b_mid, "w_out": w_out, "b_out": b_out}


epsilon = 1e-05
power_floor = 0.001
variance_floor = 0.25

def source_model(logpower, norm_gain, w_in, b_in, w_mid, b_mid, w_out, b_out):
    values = logpower.astype(jnp.float32)
    average = lax.optimization_barrier(jnp.mean(values, axis=1, keepdims=True))
    centred = values - average
    spread = lax.optimization_barrier(jnp.mean(centred * centred, axis=1, keepdims=True))
    normed = (centred * lax.rsqrt(spread + epsilon) * norm_gain).astype(jnp.bfloat16)
    hidden_one = jax.nn.silu(jnp.dot(normed, w_in, preferred_element_type=jnp.float32) + b_in).astype(jnp.bfloat16)
    hidden_two = jax.nn.silu(jnp.dot(hidden_one, w_mid, preferred_element_type=jnp.float32) + b_mid).astype(jnp.bfloat16)
    output_pre = jnp.dot(hidden_two, w_out, preferred_element_type=jnp.float32) + b_out
    return (jax.nn.softplus(output_pre) + variance_floor).astype(jnp.bfloat16)

def reference(spectra, norm_gain, w_in, b_in, w_mid, b_mid, w_out, b_out):
    real_part = spectra[0].astype(jnp.float32)
    imag_part = spectra[1].astype(jnp.float32)
    logpower = jnp.log(real_part * real_part + imag_part * imag_part + power_floor).astype(jnp.bfloat16)

    def per_source(sheet):
        return source_model(sheet.T, norm_gain, w_in, b_in, w_mid, b_mid, w_out, b_out).T
    variances = lax.map(per_source, logpower)
    weight = 1.0 / variances.astype(jnp.float32)
    frames = spectra.shape[3]
    count = spectra.shape[1]

    def sweep(source, carry):
        demix_real, demix_imag = carry
        pick_real = lax.dynamic_index_in_dim(demix_real, source, 0, keepdims=False)
        pick_imag = lax.dynamic_index_in_dim(demix_imag, source, 0, keepdims=False)
        numer_real = lax.optimization_barrier(jnp.sum(weight * (demix_real * pick_real + demix_imag * pick_imag), axis=2)) / frames
        numer_imag = lax.optimization_barrier(jnp.sum(weight * (demix_imag * pick_real - demix_real * pick_imag), axis=2)) / frames
        denom = lax.optimization_barrier(jnp.sum(weight * (pick_real * pick_real + pick_imag * pick_imag), axis=2)) / frames
        is_self = (jnp.arange(count, dtype=jnp.int32) == source)[:, None]
        coef_real = jnp.where(is_self, 1.0 - lax.rsqrt(denom), numer_real / denom)[:, :, None]
        coef_imag = jnp.where(is_self, 0.0, numer_imag / denom)[:, :, None]
        new_real = demix_real - (coef_real * pick_real - coef_imag * pick_imag)
        new_imag = demix_imag - (coef_real * pick_imag + coef_imag * pick_real)
        return (new_real, new_imag)
    demix_real, demix_imag = lax.fori_loop(0, count, sweep, (real_part, imag_part))
    return (jnp.stack([demix_real, demix_imag]), variances)
```

```python
import jax
import jax.numpy as jnp
from jax import lax
from jax.sharding import PartitionSpec as P

epsilon = 1e-05
power_floor = 0.001
variance_floor = 0.25


def coefficients(numer_real, numer_imag, denom, source, count):
    is_self = (jnp.arange(count, dtype=jnp.int32) == source)[:, None]
    coef_real = jnp.where(is_self, 1.0 - lax.rsqrt(denom), numer_real / denom)
    coef_imag = jnp.where(is_self, 0.0, numer_imag / denom)
    return (coef_real, coef_imag)


def source_model(spectra, norm_gain, w_in, b_in, w_mid, b_mid, w_out, b_out):
    real_part = spectra[0].astype(jnp.float32)
    imag_part = spectra[1].astype(jnp.float32)
    logpower = jnp.log(real_part * real_part + imag_part * imag_part + power_floor).astype(
        jnp.bfloat16
    )
    values = lax.all_to_all(logpower, "freq", split_axis=2, concat_axis=1, tiled=True).astype(
        jnp.float32
    )
    average = jnp.mean(values, axis=1, keepdims=True)
    centred = values - average
    spread = jnp.mean(centred * centred, axis=1, keepdims=True)
    normed = (centred * lax.rsqrt(spread + epsilon) * norm_gain[None, :, None]).astype(jnp.bfloat16)
    hidden_one = jax.nn.silu(
        jnp.einsum("nft,fh->nth", normed, w_in, preferred_element_type=jnp.float32) + b_in
    ).astype(jnp.bfloat16)
    hidden_two = jax.nn.silu(
        jnp.einsum("nth,hg->ntg", hidden_one, w_mid, preferred_element_type=jnp.float32) + b_mid
    ).astype(jnp.bfloat16)
    output_pre = (
        jnp.einsum("nth,hf->nft", hidden_two, w_out, preferred_element_type=jnp.float32)
        + b_out[None, :, None]
    )
    frame_variances = (jax.nn.softplus(output_pre) + variance_floor).astype(jnp.bfloat16)
    return lax.all_to_all(frame_variances, "freq", split_axis=1, concat_axis=2, tiled=True)


def on_device(spectra, norm_gain, w_in, b_in, w_mid, b_mid, w_out, b_out):
    count = spectra.shape[1]
    frames = spectra.shape[3] * lax.axis_size("frame")
    variances = source_model(spectra, norm_gain, w_in, b_in, w_mid, b_mid, w_out, b_out)

    spec_sw = lax.all_to_all(spectra, "frame", split_axis=2, concat_axis=3, tiled=True)
    var_sw = lax.all_to_all(variances, "frame", split_axis=1, concat_axis=2, tiled=True)
    weight = 1.0 / var_sw.astype(jnp.float32)
    bins = spec_sw.shape[2]
    eye = jnp.broadcast_to(jnp.eye(count, dtype=jnp.float32)[:, :, None], (count, count, bins))

    def sweep(source, carry):
        demix_real, demix_imag, mix_real, mix_imag = carry
        pick_real = lax.dynamic_index_in_dim(demix_real, source, 0, keepdims=False)
        pick_imag = lax.dynamic_index_in_dim(demix_imag, source, 0, keepdims=False)
        numer_real = jnp.sum(weight * (demix_real * pick_real + demix_imag * pick_imag), axis=2)
        numer_imag = jnp.sum(weight * (demix_imag * pick_real - demix_real * pick_imag), axis=2)
        denom = jnp.sum(weight * (pick_real * pick_real + pick_imag * pick_imag), axis=2)
        coef_real, coef_imag = coefficients(
            numer_real / frames, numer_imag / frames, denom / frames, source, count
        )
        coef_real = coef_real[:, :, None]
        coef_imag = coef_imag[:, :, None]
        new_real = demix_real - (coef_real * pick_real - coef_imag * pick_imag)
        new_imag = demix_imag - (coef_real * pick_imag + coef_imag * pick_real)
        row_real = lax.dynamic_index_in_dim(mix_real, source, 0, keepdims=False)[None]
        row_imag = lax.dynamic_index_in_dim(mix_imag, source, 0, keepdims=False)[None]
        cr = coef_real[:, None, :, 0]
        ci = coef_imag[:, None, :, 0]
        new_mix_real = mix_real - (cr * row_real - ci * row_imag)
        new_mix_imag = mix_imag - (cr * row_imag + ci * row_real)
        return (new_real, new_imag, new_mix_real, new_mix_imag)

    init = (spec_sw[0].astype(jnp.float32), spec_sw[1].astype(jnp.float32), eye, jnp.zeros_like(eye))
    _, _, mix_real, mix_imag = lax.fori_loop(0, count, sweep, init)

    mix_real = lax.all_gather(mix_real, "frame", axis=2, tiled=True)
    mix_imag = lax.all_gather(mix_imag, "frame", axis=2, tiled=True)
    top = jnp.concatenate([mix_real, -mix_imag], axis=1)
    bottom = jnp.concatenate([mix_imag, mix_real], axis=1)
    mix = jnp.concatenate([top, bottom], axis=0)
    stacked = spectra.reshape(2 * count, spectra.shape[2], spectra.shape[3]).astype(jnp.float32)
    demixed = jnp.einsum(
        "jaf,aft->jft", mix, stacked, precision=lax.Precision.HIGHEST,
        preferred_element_type=jnp.float32,
    )
    return (demixed.reshape(spectra.shape), variances)


def solution(mesh):
    in_specs = (P(None, None, "freq", "frame"), P(), P(), P(), P(), P(), P(), P())
    out_specs = (P(None, None, "freq", "frame"), P(None, "freq", "frame"))
    return jax.shard_map(
        on_device, mesh=mesh, in_specs=in_specs, out_specs=out_specs, check_vma=False
    )
```

```python
import functools

import jax
import jax.numpy as jnp
from jax import lax
from jax.experimental import pallas as pl
from jax.experimental.pallas import tpu as pltpu
from jax.sharding import PartitionSpec as P

epsilon = 1e-05
power_floor = 0.001
variance_floor = 0.25


def source_model(spectra, norm_gain, w_in, b_in, w_mid, b_mid, w_out, b_out):
    real_part = spectra[0].astype(jnp.float32)
    imag_part = spectra[1].astype(jnp.float32)
    logpower = jnp.log(real_part * real_part + imag_part * imag_part + power_floor).astype(
        jnp.bfloat16
    )
    values = lax.all_to_all(logpower, "freq", split_axis=2, concat_axis=1, tiled=True).astype(
        jnp.float32
    )
    average = jnp.mean(values, axis=1, keepdims=True)
    centred = values - average
    spread = jnp.mean(centred * centred, axis=1, keepdims=True)
    normed = (centred * lax.rsqrt(spread + epsilon) * norm_gain[None, :, None]).astype(jnp.bfloat16)
    hidden_one = jax.nn.silu(
        jnp.einsum("nft,fh->nth", normed, w_in, preferred_element_type=jnp.float32) + b_in
    ).astype(jnp.bfloat16)
    hidden_two = jax.nn.silu(
        jnp.einsum("nth,hg->ntg", hidden_one, w_mid, preferred_element_type=jnp.float32) + b_mid
    ).astype(jnp.bfloat16)
    output_pre = (
        jnp.einsum("nth,hf->nft", hidden_two, w_out, preferred_element_type=jnp.float32)
        + b_out[None, :, None]
    )
    frame_variances = (jax.nn.softplus(output_pre) + variance_floor).astype(jnp.bfloat16)
    return lax.all_to_all(frame_variances, "freq", split_axis=1, concat_axis=2, tiled=True)


def sweep_kernel(frames, spec_ref, var_ref, mr_ref, mi_ref, yr, yi, w, pr, pi, pp):
    count, bins, length = yr.shape
    chunk = 512
    chunks = length // chunk

    def init(j, carry):
        yr[j] = spec_ref[0, j].astype(jnp.float32)
        yi[j] = spec_ref[1, j].astype(jnp.float32)
        w[j] = 1.0 / var_ref[j].astype(jnp.float32)
        lane = lax.broadcasted_iota(jnp.int32, (bins, mr_ref.shape[2]), 1)
        mr_ref[j] = jnp.where(lane == j, 1.0, 0.0).astype(jnp.float32)
        mi_ref[j] = jnp.zeros((bins, mr_ref.shape[2]), jnp.float32)
        return carry

    lax.fori_loop(0, count, init, 0)

    def step(k, carry):
        pr[...] = yr[k]
        pi[...] = yi[k]
        pp[...] = pr[...] * pr[...] + pi[...] * pi[...]
        mkr = mr_ref[k]
        mki = mi_ref[k]

        def per_source(j, carry):
            acc_r = jnp.zeros((bins, chunk), jnp.float32)
            acc_i = jnp.zeros((bins, chunk), jnp.float32)
            acc_d = jnp.zeros((bins, chunk), jnp.float32)
            for c in range(chunks):
                sl = pl.ds(c * chunk, chunk)
                a_r = yr[j, :, sl]
                a_i = yi[j, :, sl]
                ww = w[j, :, sl]
                b_r = pr[:, sl]
                b_i = pi[:, sl]
                acc_r = acc_r + ww * (a_r * b_r + a_i * b_i)
                acc_i = acc_i + ww * (a_i * b_r - a_r * b_i)
                acc_d = acc_d + ww * pp[:, sl]
            numer_real = jnp.sum(acc_r, axis=1, keepdims=True) / frames
            numer_imag = jnp.sum(acc_i, axis=1, keepdims=True) / frames
            denom = jnp.sum(acc_d, axis=1, keepdims=True) / frames
            is_self = j == k
            coef_real = jnp.where(is_self, 1.0 - lax.rsqrt(denom), numer_real / denom)
            coef_imag = jnp.where(is_self, 0.0, numer_imag / denom)
            for c in range(chunks):
                sl = pl.ds(c * chunk, chunk)
                b_r = pr[:, sl]
                b_i = pi[:, sl]
                yr[j, :, sl] = yr[j, :, sl] - (coef_real * b_r - coef_imag * b_i)
                yi[j, :, sl] = yi[j, :, sl] - (coef_real * b_i + coef_imag * b_r)
            mr_ref[j] = mr_ref[j] - (coef_real * mkr - coef_imag * mki)
            mi_ref[j] = mi_ref[j] - (coef_real * mki + coef_imag * mkr)
            return carry

        lax.fori_loop(0, count, per_source, 0)
        return carry

    lax.fori_loop(0, count, step, 0)


def sweep(spec_sw, var_sw, frames):
    _, count, bins, length = spec_sw.shape
    lanes = 128
    vmem = pl.BlockSpec(memory_space=pltpu.VMEM)
    return pl.pallas_call(
        functools.partial(sweep_kernel, frames),
        out_shape=(
            jax.ShapeDtypeStruct((count, bins, lanes), jnp.float32),
            jax.ShapeDtypeStruct((count, bins, lanes), jnp.float32),
        ),
        in_specs=[vmem, vmem],
        out_specs=(vmem, vmem),
        scratch_shapes=[
            pltpu.VMEM((count, bins, length), jnp.float32),
            pltpu.VMEM((count, bins, length), jnp.float32),
            pltpu.VMEM((count, bins, length), jnp.float32),
            pltpu.VMEM((bins, length), jnp.float32),
            pltpu.VMEM((bins, length), jnp.float32),
            pltpu.VMEM((bins, length), jnp.float32),
        ],
        compiler_params=pltpu.CompilerParams(vmem_limit_bytes=60 * 1024 * 1024),
    )(spec_sw, var_sw)


def on_device(spectra, norm_gain, w_in, b_in, w_mid, b_mid, w_out, b_out):
    count = spectra.shape[1]
    frames = spectra.shape[3] * lax.axis_size("frame")
    variances = source_model(spectra, norm_gain, w_in, b_in, w_mid, b_mid, w_out, b_out)

    spec_sw = lax.all_to_all(spectra, "frame", split_axis=2, concat_axis=3, tiled=True)
    var_sw = lax.all_to_all(variances, "frame", split_axis=1, concat_axis=2, tiled=True)
    mix_real, mix_imag = sweep(spec_sw, var_sw, frames)
    mix = jnp.stack([mix_real[:, :, :count], mix_imag[:, :, :count]])
    mix = lax.all_gather(mix, "frame", axis=2, tiled=True)
    mix_real, mix_imag = mix[0], mix[1]
    top = jnp.concatenate([mix_real, -mix_imag], axis=2)
    bottom = jnp.concatenate([mix_imag, mix_real], axis=2)
    mix = jnp.concatenate([top, bottom], axis=0)
    stacked = spectra.reshape(2 * count, spectra.shape[2], spectra.shape[3]).astype(jnp.float32)
    demixed = jnp.einsum(
        "jfa,aft->jft", mix, stacked, precision=lax.Precision.HIGHEST,
        preferred_element_type=jnp.float32,
    )
    return (demixed.reshape(spectra.shape), variances)


def solution(mesh):
    in_specs = (P(None, None, "freq", "frame"), P(), P(), P(), P(), P(), P(), P())
    out_specs = (P(None, None, "freq", "frame"), P(None, "freq", "frame"))
    return jax.shard_map(
        on_device, mesh=mesh, in_specs=in_specs, out_specs=out_specs, check_vma=False
    )
```

```python
import functools

import jax
import jax.numpy as jnp
from jax import lax
from jax.experimental import pallas as pl
from jax.experimental.pallas import tpu as pltpu
from jax.sharding import PartitionSpec as P

epsilon = 1e-05
power_floor = 0.001
variance_floor = 0.25


def source_model(spectra, norm_gain, w_in, b_in, w_mid, b_mid, w_out, b_out):
    real_part = spectra[0].astype(jnp.float32)
    imag_part = spectra[1].astype(jnp.float32)
    logpower = jnp.log(real_part * real_part + imag_part * imag_part + power_floor).astype(
        jnp.bfloat16
    )
    values = lax.all_to_all(logpower, "freq", split_axis=2, concat_axis=1, tiled=True).astype(
        jnp.float32
    )
    average = jnp.mean(values, axis=1, keepdims=True)
    centred = values - average
    spread = jnp.mean(centred * centred, axis=1, keepdims=True)
    normed = (centred * lax.rsqrt(spread + epsilon) * norm_gain[None, :, None]).astype(jnp.bfloat16)
    hidden_one = jax.nn.silu(
        jnp.einsum("nft,fh->nth", normed, w_in, preferred_element_type=jnp.float32) + b_in
    ).astype(jnp.bfloat16)
    hidden_two = jax.nn.silu(
        jnp.einsum("nth,hg->ntg", hidden_one, w_mid, preferred_element_type=jnp.float32) + b_mid
    ).astype(jnp.bfloat16)
    output_pre = (
        jnp.einsum("nth,hf->nft", hidden_two, w_out, preferred_element_type=jnp.float32)
        + b_out[None, :, None]
    )
    frame_variances = (jax.nn.softplus(output_pre) + variance_floor).astype(jnp.bfloat16)
    return lax.all_to_all(frame_variances, "freq", split_axis=1, concat_axis=2, tiled=True)


def sweep_kernel(frames, spec_ref, var_ref, mr_ref, mi_ref, yr, yi, w, pr, pi, pp):
    count, bins, length = yr.shape
    chunk = 512
    chunks = length // chunk

    def init(j, carry):
        yr[j] = spec_ref[0, j].astype(jnp.float32)
        yi[j] = spec_ref[1, j].astype(jnp.float32)
        w[j] = 1.0 / var_ref[j].astype(jnp.float32)
        lane = lax.broadcasted_iota(jnp.int32, (bins, mr_ref.shape[2]), 1)
        mr_ref[j] = jnp.where(lane == j, 1.0, 0.0).astype(jnp.float32)
        mi_ref[j] = jnp.zeros((bins, mr_ref.shape[2]), jnp.float32)
        return carry

    lax.fori_loop(0, count, init, 0)

    def step(k, carry):
        pr[...] = yr[k]
        pi[...] = yi[k]
        pp[...] = pr[...] * pr[...] + pi[...] * pi[...]
        mkr = mr_ref[k]
        mki = mi_ref[k]

        def per_source(j, carry):
            acc_r = jnp.zeros((bins, chunk), jnp.float32)
            acc_i = jnp.zeros((bins, chunk), jnp.float32)
            acc_d = jnp.zeros((bins, chunk), jnp.float32)
            for c in range(chunks):
                sl = pl.ds(c * chunk, chunk)
                a_r = yr[j, :, sl]
                a_i = yi[j, :, sl]
                ww = w[j, :, sl]
                b_r = pr[:, sl]
                b_i = pi[:, sl]
                acc_r = acc_r + ww * (a_r * b_r + a_i * b_i)
                acc_i = acc_i + ww * (a_i * b_r - a_r * b_i)
                acc_d = acc_d + ww * pp[:, sl]
            numer_real = jnp.sum(acc_r, axis=1, keepdims=True) / frames
            numer_imag = jnp.sum(acc_i, axis=1, keepdims=True) / frames
            denom = jnp.sum(acc_d, axis=1, keepdims=True) / frames
            is_self = j == k
            coef_real = jnp.where(is_self, 1.0 - lax.rsqrt(denom), numer_real / denom)
            coef_imag = jnp.where(is_self, 0.0, numer_imag / denom)
            for c in range(chunks):
                sl = pl.ds(c * chunk, chunk)
                b_r = pr[:, sl]
                b_i = pi[:, sl]
                yr[j, :, sl] = yr[j, :, sl] - (coef_real * b_r - coef_imag * b_i)
                yi[j, :, sl] = yi[j, :, sl] - (coef_real * b_i + coef_imag * b_r)
            mr_ref[j] = mr_ref[j] - (coef_real * mkr - coef_imag * mki)
            mi_ref[j] = mi_ref[j] - (coef_real * mki + coef_imag * mkr)
            return carry

        lax.fori_loop(0, count, per_source, 0)
        return carry

    lax.fori_loop(0, count, step, 0)


def sweep(spec_sw, var_sw, frames):
    _, count, bins, length = spec_sw.shape
    lanes = 128
    vmem = pl.BlockSpec(memory_space=pltpu.VMEM)
    return pl.pallas_call(
        functools.partial(sweep_kernel, frames),
        out_shape=(
            jax.ShapeDtypeStruct((count, bins, lanes), jnp.float32),
            jax.ShapeDtypeStruct((count, bins, lanes), jnp.float32),
        ),
        in_specs=[vmem, vmem],
        out_specs=(vmem, vmem),
        scratch_shapes=[
            pltpu.VMEM((count, bins, length), jnp.float32),
            pltpu.VMEM((count, bins, length), jnp.float32),
            pltpu.VMEM((count, bins, length), jnp.float32),
            pltpu.VMEM((bins, length), jnp.float32),
            pltpu.VMEM((bins, length), jnp.float32),
            pltpu.VMEM((bins, length), jnp.float32),
        ],
        compiler_params=pltpu.CompilerParams(vmem_limit_bytes=60 * 1024 * 1024),
    )(spec_sw, var_sw)


def on_device(spectra, norm_gain, w_in, b_in, w_mid, b_mid, w_out, b_out):
    count = spectra.shape[1]
    frames = spectra.shape[3] * lax.axis_size("frame")
    variances = source_model(spectra, norm_gain, w_in, b_in, w_mid, b_mid, w_out, b_out)

    both = jnp.concatenate([spectra, variances[None]], axis=0)
    both = lax.all_to_all(both, "frame", split_axis=2, concat_axis=3, tiled=True)
    spec_sw, var_sw = both[:2], both[2]
    mix_real, mix_imag = sweep(spec_sw, var_sw, frames)
    mix = jnp.stack([mix_real[:, :, :count], mix_imag[:, :, :count]])
    mix = lax.all_gather(mix, "frame", axis=2, tiled=True)
    mix_real, mix_imag = mix[0], mix[1]
    top = jnp.concatenate([mix_real, -mix_imag], axis=2)
    bottom = jnp.concatenate([mix_imag, mix_real], axis=2)
    mix = jnp.concatenate([top, bottom], axis=0)
    stacked = spectra.reshape(2 * count, spectra.shape[2], spectra.shape[3]).astype(jnp.float32)
    demixed = jnp.einsum(
        "jfa,aft->jft", mix, stacked, precision=lax.Precision.HIGHEST,
        preferred_element_type=jnp.float32,
    )
    return (demixed.reshape(spectra.shape), variances)


def solution(mesh):
    in_specs = (P(None, None, "freq", "frame"), P(), P(), P(), P(), P(), P(), P())
    out_specs = (P(None, None, "freq", "frame"), P(None, "freq", "frame"))
    return jax.shard_map(
        on_device, mesh=mesh, in_specs=in_specs, out_specs=out_specs, check_vma=False
    )
```

```python
import functools

import jax
import jax.numpy as jnp
from jax import lax
from jax.experimental import pallas as pl
from jax.experimental.pallas import tpu as pltpu
from jax.sharding import PartitionSpec as P

epsilon = 1e-05
power_floor = 0.001
variance_floor = 0.25


def source_model(spectra, norm_gain, w_in, b_in, w_mid, b_mid, w_out, b_out):
    real_part = spectra[0].astype(jnp.float32)
    imag_part = spectra[1].astype(jnp.float32)
    logpower = jnp.log(real_part * real_part + imag_part * imag_part + power_floor).astype(
        jnp.bfloat16
    )
    values = lax.all_to_all(logpower, "freq", split_axis=2, concat_axis=1, tiled=True).astype(
        jnp.float32
    )
    average = jnp.mean(values, axis=1, keepdims=True)
    centred = values - average
    spread = jnp.mean(centred * centred, axis=1, keepdims=True)
    normed = (centred * lax.rsqrt(spread + epsilon) * norm_gain[None, :, None]).astype(jnp.bfloat16)
    hidden_one = jax.nn.silu(
        jnp.einsum("nft,fh->nth", normed, w_in, preferred_element_type=jnp.float32) + b_in
    ).astype(jnp.bfloat16)
    hidden_two = jax.nn.silu(
        jnp.einsum("nth,hg->ntg", hidden_one, w_mid, preferred_element_type=jnp.float32) + b_mid
    ).astype(jnp.bfloat16)
    output_pre = (
        jnp.einsum("nth,hf->nft", hidden_two, w_out, preferred_element_type=jnp.float32)
        + b_out[None, :, None]
    )
    frame_variances = (jax.nn.softplus(output_pre) + variance_floor).astype(jnp.bfloat16)
    return lax.all_to_all(frame_variances, "freq", split_axis=1, concat_axis=2, tiled=True)


def sweep_kernel(frames, spec_ref, var_ref, mr_ref, mi_ref, yr, yi, w, pr, pi, pp):
    count, bins, length = yr.shape
    chunk = 512
    chunks = length // chunk

    def init(j, carry):
        yr[j] = spec_ref[0, j].astype(jnp.float32)
        yi[j] = spec_ref[1, j].astype(jnp.float32)
        w[j] = 1.0 / var_ref[j].astype(jnp.float32)
        lane = lax.broadcasted_iota(jnp.int32, (bins, mr_ref.shape[2]), 1)
        mr_ref[j] = jnp.where(lane == j, 1.0, 0.0).astype(jnp.float32)
        mi_ref[j] = jnp.zeros((bins, mr_ref.shape[2]), jnp.float32)
        return carry

    lax.fori_loop(0, count, init, 0)

    def step(k, carry):
        pr[...] = yr[k]
        pi[...] = yi[k]
        pp[...] = pr[...] * pr[...] + pi[...] * pi[...]
        mkr = mr_ref[k]
        mki = mi_ref[k]

        def per_source(j, carry):
            acc_r = jnp.zeros((bins, chunk), jnp.float32)
            acc_i = jnp.zeros((bins, chunk), jnp.float32)
            acc_d = jnp.zeros((bins, chunk), jnp.float32)
            for c in range(chunks):
                sl = pl.ds(c * chunk, chunk)
                a_r = yr[j, :, sl]
                a_i = yi[j, :, sl]
                ww = w[j, :, sl]
                b_r = pr[:, sl]
                b_i = pi[:, sl]
                acc_r = acc_r + ww * (a_r * b_r + a_i * b_i)
                acc_i = acc_i + ww * (a_i * b_r - a_r * b_i)
                acc_d = acc_d + ww * pp[:, sl]
            numer_real = jnp.sum(acc_r, axis=1, keepdims=True) / frames
            numer_imag = jnp.sum(acc_i, axis=1, keepdims=True) / frames
            denom = jnp.sum(acc_d, axis=1, keepdims=True) / frames
            is_self = j == k
            coef_real = jnp.where(is_self, 1.0 - lax.rsqrt(denom), numer_real / denom)
            coef_imag = jnp.where(is_self, 0.0, numer_imag / denom)
            for c in range(chunks):
                sl = pl.ds(c * chunk, chunk)
                b_r = pr[:, sl]
                b_i = pi[:, sl]
                yr[j, :, sl] = yr[j, :, sl] - (coef_real * b_r - coef_imag * b_i)
                yi[j, :, sl] = yi[j, :, sl] - (coef_real * b_i + coef_imag * b_r)
            mr_ref[j] = mr_ref[j] - (coef_real * mkr - coef_imag * mki)
            mi_ref[j] = mi_ref[j] - (coef_real * mki + coef_imag * mkr)
            return carry

        lax.fori_loop(0, count, per_source, 0)
        return carry

    lax.fori_loop(0, count, step, 0)


def sweep(spec_sw, var_sw, frames):
    _, count, bins, length = spec_sw.shape
    lanes = 128
    vmem = pl.BlockSpec(memory_space=pltpu.VMEM)
    return pl.pallas_call(
        functools.partial(sweep_kernel, frames),
        out_shape=(
            jax.ShapeDtypeStruct((count, bins, lanes), jnp.float32),
            jax.ShapeDtypeStruct((count, bins, lanes), jnp.float32),
        ),
        in_specs=[vmem, vmem],
        out_specs=(vmem, vmem),
        scratch_shapes=[
            pltpu.VMEM((count, bins, length), jnp.float32),
            pltpu.VMEM((count, bins, length), jnp.float32),
            pltpu.VMEM((count, bins, length), jnp.float32),
            pltpu.VMEM((bins, length), jnp.float32),
            pltpu.VMEM((bins, length), jnp.float32),
            pltpu.VMEM((bins, length), jnp.float32),
        ],
        compiler_params=pltpu.CompilerParams(vmem_limit_bytes=60 * 1024 * 1024),
    )(spec_sw, var_sw)


def gather_kernel(x_ref, o_ref, send_sem, recv_sem, local_sem):
    n = o_ref.shape[0]
    me = lax.axis_index("frame")
    fq = lax.axis_index("freq")
    barrier = pltpu.get_barrier_semaphore()
    for d in range(1, n):
        peer = lax.rem(me + d, n)
        pl.semaphore_signal(barrier, inc=1, device_id=(fq, peer), device_id_type=pl.DeviceIdType.MESH)
    pl.semaphore_wait(barrier, n - 1)
    local = pltpu.make_async_copy(x_ref, o_ref.at[me], local_sem)
    local.start()
    copies = []
    for d in range(1, n):
        peer = lax.rem(me + d, n)
        copy = pltpu.make_async_remote_copy(
            src_ref=x_ref, dst_ref=o_ref.at[me], send_sem=send_sem.at[d], recv_sem=recv_sem.at[d],
            device_id=(fq, peer), device_id_type=pl.DeviceIdType.MESH,
        )
        copy.start()
        copies.append(copy)
    for d in range(1, n):
        source = lax.rem(me + n - d, n)
        copies[d - 1].wait_send()
        incoming = pltpu.make_async_remote_copy(
            src_ref=x_ref, dst_ref=o_ref.at[source], send_sem=send_sem.at[d], recv_sem=recv_sem.at[d],
            device_id=(fq, source), device_id_type=pl.DeviceIdType.MESH,
        )
        incoming.wait_recv()
    local.wait()


def frame_gather(x, n):
    vmem = pl.BlockSpec(memory_space=pltpu.VMEM)
    return pl.pallas_call(
        gather_kernel,
        out_shape=jax.ShapeDtypeStruct((n,) + x.shape, x.dtype),
        in_specs=[vmem],
        out_specs=vmem,
        scratch_shapes=[
            pltpu.SemaphoreType.DMA((n,)),
            pltpu.SemaphoreType.DMA((n,)),
            pltpu.SemaphoreType.DMA,
        ],
        compiler_params=pltpu.CompilerParams(collective_id=0, has_side_effects=True),
    )(x)


def on_device(spectra, norm_gain, w_in, b_in, w_mid, b_mid, w_out, b_out):
    count = spectra.shape[1]
    frames = spectra.shape[3] * lax.axis_size("frame")
    variances = source_model(spectra, norm_gain, w_in, b_in, w_mid, b_mid, w_out, b_out)

    spec_sw = lax.all_to_all(spectra, "frame", split_axis=2, concat_axis=3, tiled=True)
    var_sw = lax.all_to_all(variances, "frame", split_axis=1, concat_axis=2, tiled=True)
    mix_real, mix_imag = sweep(spec_sw, var_sw, frames)
    mix = jnp.stack([mix_real[:, :, :count], mix_imag[:, :, :count]])
    peers = lax.axis_size("frame")
    bins = mix.shape[2]
    mix = frame_gather(mix.reshape(-1, 128), peers)
    mix = mix.reshape(peers, 2, count, bins, count).transpose(1, 2, 0, 3, 4)
    mix = mix.reshape(2, count, peers * bins, count)
    mix_real, mix_imag = mix[0], mix[1]
    top = jnp.concatenate([mix_real, -mix_imag], axis=2)
    bottom = jnp.concatenate([mix_imag, mix_real], axis=2)
    mix = jnp.concatenate([top, bottom], axis=0)
    stacked = spectra.reshape(2 * count, spectra.shape[2], spectra.shape[3]).astype(jnp.float32)
    demixed = jnp.einsum(
        "jfa,aft->jft", mix, stacked, precision=lax.Precision.HIGHEST,
        preferred_element_type=jnp.float32,
    )
    return (demixed.reshape(spectra.shape), variances)


def solution(mesh):
    in_specs = (P(None, None, "freq", "frame"), P(), P(), P(), P(), P(), P(), P())
    out_specs = (P(None, None, "freq", "frame"), P(None, "freq", "frame"))
    return jax.shard_map(
        on_device, mesh=mesh, in_specs=in_specs, out_specs=out_specs, check_vma=False
    )
```

```python
import functools

import jax
import jax.numpy as jnp
from jax import lax
from jax.experimental import pallas as pl
from jax.experimental.pallas import tpu as pltpu
from jax.sharding import PartitionSpec as P

epsilon = 1e-05
power_floor = 0.001
variance_floor = 0.25


def source_model(spectra, norm_gain, w_in, b_in, w_mid, b_mid, w_out, b_out):
    real_part = spectra[0].astype(jnp.float32)
    imag_part = spectra[1].astype(jnp.float32)
    logpower = jnp.log(real_part * real_part + imag_part * imag_part + power_floor).astype(
        jnp.bfloat16
    )
    values = lax.all_to_all(logpower, "freq", split_axis=2, concat_axis=1, tiled=True).astype(
        jnp.float32
    )
    average = jnp.mean(values, axis=1, keepdims=True)
    centred = values - average
    spread = jnp.mean(centred * centred, axis=1, keepdims=True)
    normed = (centred * lax.rsqrt(spread + epsilon) * norm_gain[None, :, None]).astype(jnp.bfloat16)
    hidden_one = jax.nn.silu(
        jnp.einsum("nft,fh->nth", normed, w_in, preferred_element_type=jnp.float32) + b_in
    ).astype(jnp.bfloat16)
    hidden_two = jax.nn.silu(
        jnp.einsum("nth,hg->ntg", hidden_one, w_mid, preferred_element_type=jnp.float32) + b_mid
    ).astype(jnp.bfloat16)
    output_pre = (
        jnp.einsum("nth,hf->nft", hidden_two, w_out, preferred_element_type=jnp.float32)
        + b_out[None, :, None]
    )
    frame_variances = (jax.nn.softplus(output_pre) + variance_floor).astype(jnp.bfloat16)
    return lax.all_to_all(frame_variances, "freq", split_axis=1, concat_axis=2, tiled=True)


def sweep_kernel(frames, spec_hbm, var_hbm, mr_ref, mi_ref, spec_in, var_in, yr, yi, w, pr, pi, pp, sems):
    count, bins, length = yr.shape
    peers, _, _, span = spec_in.shape
    chunk = 512
    chunks = length // chunk
    me = lax.axis_index("frame")
    fq = lax.axis_index("freq")
    mesh_id = pl.DeviceIdType.MESH

    barrier = pltpu.get_barrier_semaphore()
    for d in range(1, peers):
        peer = lax.rem(me + d, peers)
        pl.semaphore_signal(barrier, inc=1, device_id=(fq, peer), device_id_type=mesh_id)
    pl.semaphore_wait(barrier, peers - 1)

    def exchange(src, dst, d, kind):
        peer = lax.rem(me + d, peers)
        return pltpu.make_async_remote_copy(
            src_ref=src.at[peer], dst_ref=dst.at[me], send_sem=sems.at[kind, 0, d],
            recv_sem=sems.at[kind, 1, d], device_id=(fq, peer), device_id_type=mesh_id,
        )

    def incoming(src, dst, d, kind):
        source = lax.rem(me + peers - d, peers)
        return pltpu.make_async_remote_copy(
            src_ref=src.at[source], dst_ref=dst.at[source], send_sem=sems.at[kind, 0, d],
            recv_sem=sems.at[kind, 1, d], device_id=(fq, source), device_id_type=mesh_id,
        )

    local_spec = pltpu.make_async_copy(spec_hbm.at[me], spec_in.at[me], sems.at[0, 0, 0])
    local_var = pltpu.make_async_copy(var_hbm.at[me], var_in.at[me], sems.at[1, 0, 0])
    local_spec.start()
    local_var.start()
    sends = []
    for d in range(1, peers):
        for kind, (src, dst) in enumerate(((spec_hbm, spec_in), (var_hbm, var_in))):
            copy = exchange(src, dst, d, kind)
            copy.start()
            sends.append(copy)
    for copy in sends:
        copy.wait_send()
    for d in range(1, peers):
        incoming(spec_hbm, spec_in, d, 0).wait_recv()
        incoming(var_hbm, var_in, d, 1).wait_recv()
    local_spec.wait()
    local_var.wait()

    def init(s, carry):
        cols = pl.ds(pl.multiple_of(s * span, span), span)

        def per_pair(p, carry):
            block = var_in[s, p].astype(jnp.float32)
            w[2 * p, :, cols] = 1.0 / block[:bins]
            w[2 * p + 1, :, cols] = 1.0 / block[bins:]
            for half in range(2):
                j = 2 * p + half
                spec = spec_in[s, j].astype(jnp.float32)
                yr[j, :, cols] = spec[:bins]
                yi[j, :, cols] = spec[bins:]
            return carry

        lax.fori_loop(0, count // 2, per_pair, 0)
        return carry

    lax.fori_loop(0, peers, init, 0)

    def init_mix(j, carry):
        lane = lax.broadcasted_iota(jnp.int32, (bins, mr_ref.shape[2]), 1)
        mr_ref[j] = jnp.where(lane == j, 1.0, 0.0).astype(jnp.float32)
        mi_ref[j] = jnp.zeros((bins, mr_ref.shape[2]), jnp.float32)
        return carry

    lax.fori_loop(0, count, init_mix, 0)

    def step(k, carry):
        pr[...] = yr[k]
        pi[...] = yi[k]
        pp[...] = pr[...] * pr[...] + pi[...] * pi[...]
        mkr = mr_ref[k]
        mki = mi_ref[k]

        def per_source(j, carry):
            acc_r = jnp.zeros((bins, chunk), jnp.float32)
            acc_i = jnp.zeros((bins, chunk), jnp.float32)
            acc_d = jnp.zeros((bins, chunk), jnp.float32)
            for c in range(chunks):
                sl = pl.ds(c * chunk, chunk)
                a_r = yr[j, :, sl]
                a_i = yi[j, :, sl]
                ww = w[j, :, sl]
                b_r = pr[:, sl]
                b_i = pi[:, sl]
                acc_r = acc_r + ww * (a_r * b_r + a_i * b_i)
                acc_i = acc_i + ww * (a_i * b_r - a_r * b_i)
                acc_d = acc_d + ww * pp[:, sl]
            numer_real = jnp.sum(acc_r, axis=1, keepdims=True) / frames
            numer_imag = jnp.sum(acc_i, axis=1, keepdims=True) / frames
            denom = jnp.sum(acc_d, axis=1, keepdims=True) / frames
            is_self = j == k
            coef_real = jnp.where(is_self, 1.0 - lax.rsqrt(denom), numer_real / denom)
            coef_imag = jnp.where(is_self, 0.0, numer_imag / denom)
            for c in range(chunks):
                sl = pl.ds(c * chunk, chunk)
                b_r = pr[:, sl]
                b_i = pi[:, sl]
                yr[j, :, sl] = yr[j, :, sl] - (coef_real * b_r - coef_imag * b_i)
                yi[j, :, sl] = yi[j, :, sl] - (coef_real * b_i + coef_imag * b_r)
            mr_ref[j] = mr_ref[j] - (coef_real * mkr - coef_imag * mki)
            mi_ref[j] = mi_ref[j] - (coef_real * mki + coef_imag * mkr)
            return carry

        lax.fori_loop(0, count, per_source, 0)
        return carry

    lax.fori_loop(0, count, step, 0)


def sweep(spectra, variances, frames):
    _, count, freq, span = spectra.shape
    peers = frames // span
    bins = freq // peers
    spec_send = spectra.reshape(2, count, peers, bins, span).transpose(2, 1, 0, 3, 4)
    spec_send = spec_send.reshape(peers, count, 2 * bins, span)
    var_send = variances.reshape(count // 2, 2, peers, bins, span).transpose(2, 0, 1, 3, 4)
    var_send = var_send.reshape(peers, count // 2, 2 * bins, span)
    lanes = 128
    vmem = pl.BlockSpec(memory_space=pltpu.VMEM)
    anywhere = pl.BlockSpec(memory_space=pl.ANY)
    return pl.pallas_call(
        functools.partial(sweep_kernel, frames),
        out_shape=(
            jax.ShapeDtypeStruct((count, bins, lanes), jnp.float32),
            jax.ShapeDtypeStruct((count, bins, lanes), jnp.float32),
        ),
        in_specs=[anywhere, anywhere],
        out_specs=(vmem, vmem),
        scratch_shapes=[
            pltpu.VMEM((peers, count, 2 * bins, span), spectra.dtype),
            pltpu.VMEM((peers, count // 2, 2 * bins, span), variances.dtype),
            pltpu.VMEM((count, bins, frames), jnp.float32),
            pltpu.VMEM((count, bins, frames), jnp.float32),
            pltpu.VMEM((count, bins, frames), jnp.float32),
            pltpu.VMEM((bins, frames), jnp.float32),
            pltpu.VMEM((bins, frames), jnp.float32),
            pltpu.VMEM((bins, frames), jnp.float32),
            pltpu.SemaphoreType.DMA((2, 2, peers)),
        ],
        compiler_params=pltpu.CompilerParams(
            collective_id=1, has_side_effects=True, vmem_limit_bytes=60 * 1024 * 1024
        ),
    )(spec_send, var_send)


def gather_kernel(x_ref, o_ref, send_sem, recv_sem, local_sem):
    n = o_ref.shape[0]
    me = lax.axis_index("frame")
    fq = lax.axis_index("freq")
    barrier = pltpu.get_barrier_semaphore()
    for d in range(1, n):
        peer = lax.rem(me + d, n)
        pl.semaphore_signal(barrier, inc=1, device_id=(fq, peer), device_id_type=pl.DeviceIdType.MESH)
    pl.semaphore_wait(barrier, n - 1)
    local = pltpu.make_async_copy(x_ref, o_ref.at[me], local_sem)
    local.start()
    copies = []
    for d in range(1, n):
        peer = lax.rem(me + d, n)
        copy = pltpu.make_async_remote_copy(
            src_ref=x_ref, dst_ref=o_ref.at[me], send_sem=send_sem.at[d], recv_sem=recv_sem.at[d],
            device_id=(fq, peer), device_id_type=pl.DeviceIdType.MESH,
        )
        copy.start()
        copies.append(copy)
    for d in range(1, n):
        source = lax.rem(me + n - d, n)
        copies[d - 1].wait_send()
        incoming = pltpu.make_async_remote_copy(
            src_ref=x_ref, dst_ref=o_ref.at[source], send_sem=send_sem.at[d], recv_sem=recv_sem.at[d],
            device_id=(fq, source), device_id_type=pl.DeviceIdType.MESH,
        )
        incoming.wait_recv()
    local.wait()


def frame_gather(x, n):
    vmem = pl.BlockSpec(memory_space=pltpu.VMEM)
    return pl.pallas_call(
        gather_kernel,
        out_shape=jax.ShapeDtypeStruct((n,) + x.shape, x.dtype),
        in_specs=[vmem],
        out_specs=vmem,
        scratch_shapes=[
            pltpu.SemaphoreType.DMA((n,)),
            pltpu.SemaphoreType.DMA((n,)),
            pltpu.SemaphoreType.DMA,
        ],
        compiler_params=pltpu.CompilerParams(collective_id=0, has_side_effects=True),
    )(x)


def on_device(spectra, norm_gain, w_in, b_in, w_mid, b_mid, w_out, b_out):
    count = spectra.shape[1]
    frames = spectra.shape[3] * lax.axis_size("frame")
    variances = source_model(spectra, norm_gain, w_in, b_in, w_mid, b_mid, w_out, b_out)

    mix_real, mix_imag = sweep(spectra, variances, frames)
    mix = jnp.stack([mix_real[:, :, :count], mix_imag[:, :, :count]])
    peers = lax.axis_size("frame")
    bins = mix.shape[2]
    mix = frame_gather(mix.reshape(-1, 128), peers)
    mix = mix.reshape(peers, 2, count, bins, count).transpose(1, 2, 0, 3, 4)
    mix = mix.reshape(2, count, peers * bins, count)
    mix_real, mix_imag = mix[0], mix[1]
    top = jnp.concatenate([mix_real, -mix_imag], axis=2)
    bottom = jnp.concatenate([mix_imag, mix_real], axis=2)
    mix = jnp.concatenate([top, bottom], axis=0)
    stacked = spectra.reshape(2 * count, spectra.shape[2], spectra.shape[3]).astype(jnp.float32)
    demixed = jnp.einsum(
        "jfa,aft->jft", mix, stacked, precision=lax.Precision.HIGHEST,
        preferred_element_type=jnp.float32,
    )
    return (demixed.reshape(spectra.shape), variances)


def solution(mesh):
    in_specs = (P(None, None, "freq", "frame"), P(), P(), P(), P(), P(), P(), P())
    out_specs = (P(None, None, "freq", "frame"), P(None, "freq", "frame"))
    return jax.shard_map(
        on_device, mesh=mesh, in_specs=in_specs, out_specs=out_specs, check_vma=False
    )
```

```python
import functools

import jax
import jax.numpy as jnp
from jax import lax
from jax.experimental import pallas as pl
from jax.experimental.pallas import tpu as pltpu
from jax.sharding import PartitionSpec as P

epsilon = 1e-05
power_floor = 0.001
variance_floor = 0.25


def source_model(spectra, norm_gain, w_in, b_in, w_mid, b_mid, w_out, b_out):
    real_part = spectra[0].astype(jnp.float32)
    imag_part = spectra[1].astype(jnp.float32)
    logpower = jnp.log(real_part * real_part + imag_part * imag_part + power_floor).astype(
        jnp.bfloat16
    )
    values = lax.all_to_all(logpower, "freq", split_axis=2, concat_axis=1, tiled=True).astype(
        jnp.float32
    )
    average = jnp.mean(values, axis=1, keepdims=True)
    centred = values - average
    spread = jnp.mean(centred * centred, axis=1, keepdims=True)
    normed = (centred * lax.rsqrt(spread + epsilon) * norm_gain[None, :, None]).astype(jnp.bfloat16)
    hidden_one = jax.nn.silu(
        jnp.einsum("nft,fh->nth", normed, w_in, preferred_element_type=jnp.float32) + b_in
    ).astype(jnp.bfloat16)
    hidden_two = jax.nn.silu(
        jnp.einsum("nth,hg->ntg", hidden_one, w_mid, preferred_element_type=jnp.float32) + b_mid
    ).astype(jnp.bfloat16)
    output_pre = (
        jnp.einsum("nth,hf->nft", hidden_two, w_out, preferred_element_type=jnp.float32)
        + b_out[None, :, None]
    )
    frame_variances = (jax.nn.softplus(output_pre) + variance_floor).astype(jnp.bfloat16)
    return lax.all_to_all(frame_variances, "freq", split_axis=1, concat_axis=2, tiled=True)


def sweep_kernel(frames, *refs):
    peers = len(refs) - 9
    pieces = refs[:peers]
    var_ref, mr_ref, mi_ref, yr, yi, w, pr, pi, pp = refs[peers:]
    count, bins, length = yr.shape
    chunk = 512
    chunks = length // chunk

    me = lax.axis_index("frame")
    span = pieces[0].shape[2]

    def init(j, carry):
        for d in range(peers):
            source = lax.rem(me + peers - d, peers)
            cols = pl.ds(pl.multiple_of(source * span, span), span)
            spec = pieces[d][j].astype(jnp.float32)
            yr[j, :, cols] = spec[:bins]
            yi[j, :, cols] = spec[bins:]
        w[j] = 1.0 / var_ref[j].astype(jnp.float32)
        lane = lax.broadcasted_iota(jnp.int32, (bins, mr_ref.shape[2]), 1)
        mr_ref[j] = jnp.where(lane == j, 1.0, 0.0).astype(jnp.float32)
        mi_ref[j] = jnp.zeros((bins, mr_ref.shape[2]), jnp.float32)
        return carry

    lax.fori_loop(0, count, init, 0)

    def step(k, carry):
        pr[...] = yr[k]
        pi[...] = yi[k]
        pp[...] = pr[...] * pr[...] + pi[...] * pi[...]
        mkr = mr_ref[k]
        mki = mi_ref[k]

        def per_source(j, carry):
            acc_r = jnp.zeros((bins, chunk), jnp.float32)
            acc_i = jnp.zeros((bins, chunk), jnp.float32)
            acc_d = jnp.zeros((bins, chunk), jnp.float32)
            for c in range(chunks):
                sl = pl.ds(c * chunk, chunk)
                a_r = yr[j, :, sl]
                a_i = yi[j, :, sl]
                ww = w[j, :, sl]
                b_r = pr[:, sl]
                b_i = pi[:, sl]
                acc_r = acc_r + ww * (a_r * b_r + a_i * b_i)
                acc_i = acc_i + ww * (a_i * b_r - a_r * b_i)
                acc_d = acc_d + ww * pp[:, sl]
            numer_real = jnp.sum(acc_r, axis=1, keepdims=True) / frames
            numer_imag = jnp.sum(acc_i, axis=1, keepdims=True) / frames
            denom = jnp.sum(acc_d, axis=1, keepdims=True) / frames
            is_self = j == k
            coef_real = jnp.where(is_self, 1.0 - lax.rsqrt(denom), numer_real / denom)
            coef_imag = jnp.where(is_self, 0.0, numer_imag / denom)
            for c in range(chunks):
                sl = pl.ds(c * chunk, chunk)
                b_r = pr[:, sl]
                b_i = pi[:, sl]
                yr[j, :, sl] = yr[j, :, sl] - (coef_real * b_r - coef_imag * b_i)
                yi[j, :, sl] = yi[j, :, sl] - (coef_real * b_i + coef_imag * b_r)
            mr_ref[j] = mr_ref[j] - (coef_real * mkr - coef_imag * mki)
            mi_ref[j] = mi_ref[j] - (coef_real * mki + coef_imag * mkr)
            return carry

        lax.fori_loop(0, count, per_source, 0)
        return carry

    lax.fori_loop(0, count, step, 0)


def sweep(pieces, var_sw, frames):
    count, bins, length = var_sw.shape
    lanes = 128
    vmem = pl.BlockSpec(memory_space=pltpu.VMEM)
    return pl.pallas_call(
        functools.partial(sweep_kernel, frames),
        out_shape=(
            jax.ShapeDtypeStruct((count, bins, lanes), jnp.float32),
            jax.ShapeDtypeStruct((count, bins, lanes), jnp.float32),
        ),
        in_specs=[vmem] * (len(pieces) + 1),
        out_specs=(vmem, vmem),
        scratch_shapes=[
            pltpu.VMEM((count, bins, length), jnp.float32),
            pltpu.VMEM((count, bins, length), jnp.float32),
            pltpu.VMEM((count, bins, length), jnp.float32),
            pltpu.VMEM((bins, length), jnp.float32),
            pltpu.VMEM((bins, length), jnp.float32),
            pltpu.VMEM((bins, length), jnp.float32),
        ],
        compiler_params=pltpu.CompilerParams(vmem_limit_bytes=60 * 1024 * 1024),
    )(*pieces, var_sw)


def gather_kernel(x_ref, o_ref, send_sem, recv_sem, local_sem):
    n = o_ref.shape[0]
    me = lax.axis_index("frame")
    fq = lax.axis_index("freq")
    barrier = pltpu.get_barrier_semaphore()
    for d in range(1, n):
        peer = lax.rem(me + d, n)
        pl.semaphore_signal(barrier, inc=1, device_id=(fq, peer), device_id_type=pl.DeviceIdType.MESH)
    pl.semaphore_wait(barrier, n - 1)
    local = pltpu.make_async_copy(x_ref, o_ref.at[me], local_sem)
    local.start()
    copies = []
    for d in range(1, n):
        peer = lax.rem(me + d, n)
        copy = pltpu.make_async_remote_copy(
            src_ref=x_ref, dst_ref=o_ref.at[me], send_sem=send_sem.at[d], recv_sem=recv_sem.at[d],
            device_id=(fq, peer), device_id_type=pl.DeviceIdType.MESH,
        )
        copy.start()
        copies.append(copy)
    for d in range(1, n):
        source = lax.rem(me + n - d, n)
        copies[d - 1].wait_send()
        incoming = pltpu.make_async_remote_copy(
            src_ref=x_ref, dst_ref=o_ref.at[source], send_sem=send_sem.at[d], recv_sem=recv_sem.at[d],
            device_id=(fq, source), device_id_type=pl.DeviceIdType.MESH,
        )
        incoming.wait_recv()
    local.wait()


def frame_gather(x, n):
    vmem = pl.BlockSpec(memory_space=pltpu.VMEM)
    return pl.pallas_call(
        gather_kernel,
        out_shape=jax.ShapeDtypeStruct((n,) + x.shape, x.dtype),
        in_specs=[vmem],
        out_specs=vmem,
        scratch_shapes=[
            pltpu.SemaphoreType.DMA((n,)),
            pltpu.SemaphoreType.DMA((n,)),
            pltpu.SemaphoreType.DMA,
        ],
        compiler_params=pltpu.CompilerParams(collective_id=0, has_side_effects=True),
    )(x)


def on_device(spectra, norm_gain, w_in, b_in, w_mid, b_mid, w_out, b_out):
    count = spectra.shape[1]
    frames = spectra.shape[3] * lax.axis_size("frame")
    peers = lax.axis_size("frame")
    me = lax.axis_index("frame")
    span = spectra.shape[3]
    bins = spectra.shape[2] // peers
    send = spectra.reshape(2, count, peers, bins, span).transpose(2, 1, 0, 3, 4)
    send = send.reshape(peers, count, 2 * bins, span)
    pieces = []
    for d in range(peers):
        piece = lax.dynamic_index_in_dim(send, lax.rem(me + d, peers), 0, keepdims=False)
        if d:
            piece = lax.ppermute(piece, "frame", [(i, (i + d) % peers) for i in range(peers)])
        pieces.append(piece)
    variances = source_model(spectra, norm_gain, w_in, b_in, w_mid, b_mid, w_out, b_out)
    var_sw = lax.all_to_all(variances, "frame", split_axis=1, concat_axis=2, tiled=True)
    mix_real, mix_imag = sweep(pieces, var_sw, frames)
    mix = jnp.stack([mix_real[:, :, :count], mix_imag[:, :, :count]])
    peers = lax.axis_size("frame")
    bins = mix.shape[2]
    mix = frame_gather(mix.reshape(-1, 128), peers)
    mix = mix.reshape(peers, 2, count, bins, count).transpose(1, 2, 0, 3, 4)
    mix = mix.reshape(2, count, peers * bins, count)
    mix_real, mix_imag = mix[0], mix[1]
    top = jnp.concatenate([mix_real, -mix_imag], axis=2)
    bottom = jnp.concatenate([mix_imag, mix_real], axis=2)
    mix = jnp.concatenate([top, bottom], axis=0)
    stacked = spectra.reshape(2 * count, spectra.shape[2], spectra.shape[3]).astype(jnp.float32)
    demixed = jnp.einsum(
        "jfa,aft->jft", mix, stacked, precision=lax.Precision.HIGHEST,
        preferred_element_type=jnp.float32,
    )
    return (demixed.reshape(spectra.shape), variances)


def solution(mesh):
    in_specs = (P(None, None, "freq", "frame"), P(), P(), P(), P(), P(), P(), P())
    out_specs = (P(None, None, "freq", "frame"), P(None, "freq", "frame"))
    return jax.shard_map(
        on_device, mesh=mesh, in_specs=in_specs, out_specs=out_specs, check_vma=False
    )
```

```python
import functools

import jax
import jax.numpy as jnp
from jax import lax
from jax.experimental import pallas as pl
from jax.experimental.pallas import tpu as pltpu
from jax.sharding import PartitionSpec as P

epsilon = 1e-05
power_floor = 0.001
variance_floor = 0.25


def source_model(spectra, norm_gain, w_in, b_in, w_mid, b_mid, w_out, b_out):
    real_part = spectra[0].astype(jnp.float32)
    imag_part = spectra[1].astype(jnp.float32)
    logpower = jnp.log(real_part * real_part + imag_part * imag_part + power_floor).astype(
        jnp.bfloat16
    )
    values = lax.all_to_all(logpower, "freq", split_axis=2, concat_axis=1, tiled=True).astype(
        jnp.float32
    )
    average = jnp.mean(values, axis=1, keepdims=True)
    centred = values - average
    spread = jnp.mean(centred * centred, axis=1, keepdims=True)
    normed = (centred * lax.rsqrt(spread + epsilon) * norm_gain[None, :, None]).astype(jnp.bfloat16)
    hidden_one = jax.nn.silu(
        jnp.einsum("nft,fh->nth", normed, w_in, preferred_element_type=jnp.float32) + b_in
    ).astype(jnp.bfloat16)
    hidden_two = jax.nn.silu(
        jnp.einsum("nth,hg->ntg", hidden_one, w_mid, preferred_element_type=jnp.float32) + b_mid
    ).astype(jnp.bfloat16)
    output_pre = (
        jnp.einsum("nth,hf->nft", hidden_two, w_out, preferred_element_type=jnp.float32)
        + b_out[None, :, None]
    )
    frame_variances = (jax.nn.softplus(output_pre) + variance_floor).astype(jnp.bfloat16)
    return lax.all_to_all(frame_variances, "freq", split_axis=1, concat_axis=2, tiled=True)


def sweep_kernel(frames, spec_in, var_in, mr_ref, mi_ref, yr, yi, w, pr, pi, pp):
    count, bins, length = yr.shape
    peers, _, _, span = spec_in.shape
    chunk = 512
    chunks = length // chunk

    def init(s, carry):
        cols = pl.ds(pl.multiple_of(s * span, span), span)

        def per_pair(p, carry):
            block = var_in[s, p].astype(jnp.float32)
            w[2 * p, :, cols] = 1.0 / block[:bins]
            w[2 * p + 1, :, cols] = 1.0 / block[bins:]
            for half in range(2):
                j = 2 * p + half
                spec = spec_in[s, j].astype(jnp.float32)
                yr[j, :, cols] = spec[:bins]
                yi[j, :, cols] = spec[bins:]
            return carry

        lax.fori_loop(0, count // 2, per_pair, 0)
        return carry

    lax.fori_loop(0, peers, init, 0)

    def init_mix(j, carry):
        lane = lax.broadcasted_iota(jnp.int32, (bins, mr_ref.shape[2]), 1)
        mr_ref[j] = jnp.where(lane == j, 1.0, 0.0).astype(jnp.float32)
        mi_ref[j] = jnp.zeros((bins, mr_ref.shape[2]), jnp.float32)
        return carry

    lax.fori_loop(0, count, init_mix, 0)

    def step(k, carry):
        pr[...] = yr[k]
        pi[...] = yi[k]
        pp[...] = pr[...] * pr[...] + pi[...] * pi[...]
        mkr = mr_ref[k]
        mki = mi_ref[k]

        def per_source(j, carry):
            acc_r = jnp.zeros((bins, chunk), jnp.float32)
            acc_i = jnp.zeros((bins, chunk), jnp.float32)
            acc_d = jnp.zeros((bins, chunk), jnp.float32)
            for c in range(chunks):
                sl = pl.ds(c * chunk, chunk)
                a_r = yr[j, :, sl]
                a_i = yi[j, :, sl]
                ww = w[j, :, sl]
                b_r = pr[:, sl]
                b_i = pi[:, sl]
                acc_r = acc_r + ww * (a_r * b_r + a_i * b_i)
                acc_i = acc_i + ww * (a_i * b_r - a_r * b_i)
                acc_d = acc_d + ww * pp[:, sl]
            numer_real = jnp.sum(acc_r, axis=1, keepdims=True) / frames
            numer_imag = jnp.sum(acc_i, axis=1, keepdims=True) / frames
            denom = jnp.sum(acc_d, axis=1, keepdims=True) / frames
            is_self = j == k
            coef_real = jnp.where(is_self, 1.0 - lax.rsqrt(denom), numer_real / denom)
            coef_imag = jnp.where(is_self, 0.0, numer_imag / denom)
            for c in range(chunks):
                sl = pl.ds(c * chunk, chunk)
                b_r = pr[:, sl]
                b_i = pi[:, sl]
                yr[j, :, sl] = yr[j, :, sl] - (coef_real * b_r - coef_imag * b_i)
                yi[j, :, sl] = yi[j, :, sl] - (coef_real * b_i + coef_imag * b_r)
            mr_ref[j] = mr_ref[j] - (coef_real * mkr - coef_imag * mki)
            mi_ref[j] = mi_ref[j] - (coef_real * mki + coef_imag * mkr)
            return carry

        lax.fori_loop(0, count, per_source, 0)
        return carry

    lax.fori_loop(0, count, step, 0)


def sweep(spec_in, var_in, frames):
    _, count, rows, _ = spec_in.shape
    bins, length = rows // 2, frames
    lanes = 128
    vmem = pl.BlockSpec(memory_space=pltpu.VMEM)
    return pl.pallas_call(
        functools.partial(sweep_kernel, frames),
        out_shape=(
            jax.ShapeDtypeStruct((count, bins, lanes), jnp.float32),
            jax.ShapeDtypeStruct((count, bins, lanes), jnp.float32),
        ),
        in_specs=[vmem, vmem],
        out_specs=(vmem, vmem),
        scratch_shapes=[
            pltpu.VMEM((count, bins, length), jnp.float32),
            pltpu.VMEM((count, bins, length), jnp.float32),
            pltpu.VMEM((count, bins, length), jnp.float32),
            pltpu.VMEM((bins, length), jnp.float32),
            pltpu.VMEM((bins, length), jnp.float32),
            pltpu.VMEM((bins, length), jnp.float32),
        ],
        compiler_params=pltpu.CompilerParams(vmem_limit_bytes=60 * 1024 * 1024),
    )(spec_in, var_in)


def gather_kernel(x_ref, o_ref, send_sem, recv_sem, local_sem):
    n = o_ref.shape[0]
    me = lax.axis_index("frame")
    fq = lax.axis_index("freq")
    barrier = pltpu.get_barrier_semaphore()
    for d in range(1, n):
        peer = lax.rem(me + d, n)
        pl.semaphore_signal(barrier, inc=1, device_id=(fq, peer), device_id_type=pl.DeviceIdType.MESH)
    pl.semaphore_wait(barrier, n - 1)
    local = pltpu.make_async_copy(x_ref, o_ref.at[me], local_sem)
    local.start()
    copies = []
    for d in range(1, n):
        peer = lax.rem(me + d, n)
        copy = pltpu.make_async_remote_copy(
            src_ref=x_ref, dst_ref=o_ref.at[me], send_sem=send_sem.at[d], recv_sem=recv_sem.at[d],
            device_id=(fq, peer), device_id_type=pl.DeviceIdType.MESH,
        )
        copy.start()
        copies.append(copy)
    for d in range(1, n):
        source = lax.rem(me + n - d, n)
        copies[d - 1].wait_send()
        incoming = pltpu.make_async_remote_copy(
            src_ref=x_ref, dst_ref=o_ref.at[source], send_sem=send_sem.at[d], recv_sem=recv_sem.at[d],
            device_id=(fq, source), device_id_type=pl.DeviceIdType.MESH,
        )
        incoming.wait_recv()
    local.wait()


def frame_gather(x, n):
    vmem = pl.BlockSpec(memory_space=pltpu.VMEM)
    return pl.pallas_call(
        gather_kernel,
        out_shape=jax.ShapeDtypeStruct((n,) + x.shape, x.dtype),
        in_specs=[vmem],
        out_specs=vmem,
        scratch_shapes=[
            pltpu.SemaphoreType.DMA((n,)),
            pltpu.SemaphoreType.DMA((n,)),
            pltpu.SemaphoreType.DMA,
        ],
        compiler_params=pltpu.CompilerParams(collective_id=0, has_side_effects=True),
    )(x)


def on_device(spectra, norm_gain, w_in, b_in, w_mid, b_mid, w_out, b_out):
    count = spectra.shape[1]
    frames = spectra.shape[3] * lax.axis_size("frame")
    variances = source_model(spectra, norm_gain, w_in, b_in, w_mid, b_mid, w_out, b_out)

    peers = lax.axis_size("frame")
    _, _, freq, span = spectra.shape
    bins = freq // peers
    spec_send = spectra.reshape(2, count, peers, bins, span).transpose(2, 1, 0, 3, 4)
    spec_send = spec_send.reshape(peers, count, 2 * bins, span)
    var_send = variances.reshape(count // 2, 2, peers, bins, span).transpose(2, 0, 1, 3, 4)
    var_send = var_send.reshape(peers, count // 2, 2 * bins, span)
    spec_in = lax.all_to_all(spec_send, "frame", split_axis=0, concat_axis=0, tiled=True)
    var_in = lax.all_to_all(var_send, "frame", split_axis=0, concat_axis=0, tiled=True)
    mix_real, mix_imag = sweep(spec_in, var_in, frames)
    mix = jnp.stack([mix_real[:, :, :count], mix_imag[:, :, :count]])
    peers = lax.axis_size("frame")
    bins = mix.shape[2]
    mix = frame_gather(mix.reshape(-1, 128), peers)
    mix = mix.reshape(peers, 2, count, bins, count).transpose(1, 2, 0, 3, 4)
    mix = mix.reshape(2, count, peers * bins, count)
    mix_real, mix_imag = mix[0], mix[1]
    top = jnp.concatenate([mix_real, -mix_imag], axis=2)
    bottom = jnp.concatenate([mix_imag, mix_real], axis=2)
    mix = jnp.concatenate([top, bottom], axis=0)
    stacked = spectra.reshape(2 * count, spectra.shape[2], spectra.shape[3]).astype(jnp.float32)
    demixed = jnp.einsum(
        "jfa,aft->jft", mix, stacked, precision=lax.Precision.HIGHEST,
        preferred_element_type=jnp.float32,
    )
    return (demixed.reshape(spectra.shape), variances)


def solution(mesh):
    in_specs = (P(None, None, "freq", "frame"), P(), P(), P(), P(), P(), P(), P())
    out_specs = (P(None, None, "freq", "frame"), P(None, "freq", "frame"))
    return jax.shard_map(
        on_device, mesh=mesh, in_specs=in_specs, out_specs=out_specs, check_vma=False
    )
```

```python
import functools

import jax
import jax.numpy as jnp
from jax import lax
from jax.experimental import pallas as pl
from jax.experimental.pallas import tpu as pltpu
from jax.sharding import PartitionSpec as P

epsilon = 1e-05
power_floor = 0.001
variance_floor = 0.25


def source_model(spectra, norm_gain, w_in, b_in, w_mid, b_mid, w_out, b_out):
    real_part = spectra[0].astype(jnp.float32)
    imag_part = spectra[1].astype(jnp.float32)
    logpower = jnp.log(real_part * real_part + imag_part * imag_part + power_floor).astype(
        jnp.bfloat16
    )
    count, freq, span = logpower.shape
    shards = lax.axis_size("freq")
    rows = span // shards
    send = logpower.transpose(0, 2, 1).reshape(count, shards, rows, freq).transpose(1, 0, 2, 3)
    received = lax.all_to_all(send, "freq", split_axis=0, concat_axis=0, tiled=True)
    values = received.transpose(1, 2, 0, 3).reshape(count, rows, shards * freq).astype(jnp.float32)
    average = jnp.mean(values, axis=2, keepdims=True)
    centred = values - average
    spread = jnp.mean(centred * centred, axis=2, keepdims=True)
    normed = (centred * lax.rsqrt(spread + epsilon) * norm_gain).astype(jnp.bfloat16)
    hidden_one = jax.nn.silu(
        jnp.einsum("ntf,fh->nth", normed, w_in, preferred_element_type=jnp.float32) + b_in
    ).astype(jnp.bfloat16)
    hidden_two = jax.nn.silu(
        jnp.einsum("nth,hg->ntg", hidden_one, w_mid, preferred_element_type=jnp.float32) + b_mid
    ).astype(jnp.bfloat16)
    output_pre = (
        jnp.einsum("nth,hf->ntf", hidden_two, w_out, preferred_element_type=jnp.float32) + b_out
    )
    frame_variances = (jax.nn.softplus(output_pre) + variance_floor).astype(jnp.bfloat16)
    send = frame_variances.reshape(count, rows, shards, freq).transpose(2, 0, 1, 3)
    received = lax.all_to_all(send, "freq", split_axis=0, concat_axis=0, tiled=True)
    return received.transpose(1, 3, 0, 2).reshape(count, freq, span)


def sweep_kernel(frames, spec_in, var_in, mr_ref, mi_ref, yr, yi, w, pr, pi, pp):
    count, bins, length = yr.shape
    peers, _, _, span = spec_in.shape
    chunk = 512
    chunks = length // chunk

    def init(s, carry):
        cols = pl.ds(pl.multiple_of(s * span, span), span)

        def per_pair(p, carry):
            block = var_in[s, p].astype(jnp.float32)
            w[2 * p, :, cols] = 1.0 / block[:bins]
            w[2 * p + 1, :, cols] = 1.0 / block[bins:]
            for half in range(2):
                j = 2 * p + half
                spec = spec_in[s, j].astype(jnp.float32)
                yr[j, :, cols] = spec[:bins]
                yi[j, :, cols] = spec[bins:]
            return carry

        lax.fori_loop(0, count // 2, per_pair, 0)
        return carry

    lax.fori_loop(0, peers, init, 0)

    def init_mix(j, carry):
        lane = lax.broadcasted_iota(jnp.int32, (bins, mr_ref.shape[2]), 1)
        mr_ref[j] = jnp.where(lane == j, 1.0, 0.0).astype(jnp.float32)
        mi_ref[j] = jnp.zeros((bins, mr_ref.shape[2]), jnp.float32)
        return carry

    lax.fori_loop(0, count, init_mix, 0)

    def step(k, carry):
        pr[...] = yr[k]
        pi[...] = yi[k]
        pp[...] = pr[...] * pr[...] + pi[...] * pi[...]
        mkr = mr_ref[k]
        mki = mi_ref[k]

        def per_source(j, carry):
            acc_r = jnp.zeros((bins, chunk), jnp.float32)
            acc_i = jnp.zeros((bins, chunk), jnp.float32)
            acc_d = jnp.zeros((bins, chunk), jnp.float32)
            for c in range(chunks):
                sl = pl.ds(c * chunk, chunk)
                a_r = yr[j, :, sl]
                a_i = yi[j, :, sl]
                ww = w[j, :, sl]
                b_r = pr[:, sl]
                b_i = pi[:, sl]
                acc_r = acc_r + ww * (a_r * b_r + a_i * b_i)
                acc_i = acc_i + ww * (a_i * b_r - a_r * b_i)
                acc_d = acc_d + ww * pp[:, sl]
            numer_real = jnp.sum(acc_r, axis=1, keepdims=True) / frames
            numer_imag = jnp.sum(acc_i, axis=1, keepdims=True) / frames
            denom = jnp.sum(acc_d, axis=1, keepdims=True) / frames
            is_self = j == k
            coef_real = jnp.where(is_self, 1.0 - lax.rsqrt(denom), numer_real / denom)
            coef_imag = jnp.where(is_self, 0.0, numer_imag / denom)
            for c in range(chunks):
                sl = pl.ds(c * chunk, chunk)
                b_r = pr[:, sl]
                b_i = pi[:, sl]
                yr[j, :, sl] = yr[j, :, sl] - (coef_real * b_r - coef_imag * b_i)
                yi[j, :, sl] = yi[j, :, sl] - (coef_real * b_i + coef_imag * b_r)
            mr_ref[j] = mr_ref[j] - (coef_real * mkr - coef_imag * mki)
            mi_ref[j] = mi_ref[j] - (coef_real * mki + coef_imag * mkr)
            return carry

        lax.fori_loop(0, count, per_source, 0)
        return carry

    lax.fori_loop(0, count, step, 0)


def sweep(spec_in, var_in, frames):
    _, count, rows, _ = spec_in.shape
    bins, length = rows // 2, frames
    lanes = 128
    vmem = pl.BlockSpec(memory_space=pltpu.VMEM)
    return pl.pallas_call(
        functools.partial(sweep_kernel, frames),
        out_shape=(
            jax.ShapeDtypeStruct((count, bins, lanes), jnp.float32),
            jax.ShapeDtypeStruct((count, bins, lanes), jnp.float32),
        ),
        in_specs=[vmem, vmem],
        out_specs=(vmem, vmem),
        scratch_shapes=[
            pltpu.VMEM((count, bins, length), jnp.float32),
            pltpu.VMEM((count, bins, length), jnp.float32),
            pltpu.VMEM((count, bins, length), jnp.float32),
            pltpu.VMEM((bins, length), jnp.float32),
            pltpu.VMEM((bins, length), jnp.float32),
            pltpu.VMEM((bins, length), jnp.float32),
        ],
        compiler_params=pltpu.CompilerParams(vmem_limit_bytes=60 * 1024 * 1024),
    )(spec_in, var_in)


def gather_kernel(x_ref, o_ref, send_sem, recv_sem, local_sem):
    n = o_ref.shape[0]
    me = lax.axis_index("frame")
    fq = lax.axis_index("freq")
    barrier = pltpu.get_barrier_semaphore()
    for d in range(1, n):
        peer = lax.rem(me + d, n)
        pl.semaphore_signal(barrier, inc=1, device_id=(fq, peer), device_id_type=pl.DeviceIdType.MESH)
    pl.semaphore_wait(barrier, n - 1)
    local = pltpu.make_async_copy(x_ref, o_ref.at[me], local_sem)
    local.start()
    copies = []
    for d in range(1, n):
        peer = lax.rem(me + d, n)
        copy = pltpu.make_async_remote_copy(
            src_ref=x_ref, dst_ref=o_ref.at[me], send_sem=send_sem.at[d], recv_sem=recv_sem.at[d],
            device_id=(fq, peer), device_id_type=pl.DeviceIdType.MESH,
        )
        copy.start()
        copies.append(copy)
    for d in range(1, n):
        source = lax.rem(me + n - d, n)
        copies[d - 1].wait_send()
        incoming = pltpu.make_async_remote_copy(
            src_ref=x_ref, dst_ref=o_ref.at[source], send_sem=send_sem.at[d], recv_sem=recv_sem.at[d],
            device_id=(fq, source), device_id_type=pl.DeviceIdType.MESH,
        )
        incoming.wait_recv()
    local.wait()


def frame_gather(x, n):
    vmem = pl.BlockSpec(memory_space=pltpu.VMEM)
    return pl.pallas_call(
        gather_kernel,
        out_shape=jax.ShapeDtypeStruct((n,) + x.shape, x.dtype),
        in_specs=[vmem],
        out_specs=vmem,
        scratch_shapes=[
            pltpu.SemaphoreType.DMA((n,)),
            pltpu.SemaphoreType.DMA((n,)),
            pltpu.SemaphoreType.DMA,
        ],
        compiler_params=pltpu.CompilerParams(collective_id=0, has_side_effects=True),
    )(x)


def on_device(spectra, norm_gain, w_in, b_in, w_mid, b_mid, w_out, b_out):
    count = spectra.shape[1]
    frames = spectra.shape[3] * lax.axis_size("frame")
    variances = source_model(spectra, norm_gain, w_in, b_in, w_mid, b_mid, w_out, b_out)

    peers = lax.axis_size("frame")
    _, _, freq, span = spectra.shape
    bins = freq // peers
    spec_send = spectra.reshape(2, count, peers, bins, span).transpose(2, 1, 0, 3, 4)
    spec_send = spec_send.reshape(peers, count, 2 * bins, span)
    var_send = variances.reshape(count // 2, 2, peers, bins, span).transpose(2, 0, 1, 3, 4)
    var_send = var_send.reshape(peers, count // 2, 2 * bins, span)
    spec_in = lax.all_to_all(spec_send, "frame", split_axis=0, concat_axis=0, tiled=True)
    var_in = lax.all_to_all(var_send, "frame", split_axis=0, concat_axis=0, tiled=True)
    mix_real, mix_imag = sweep(spec_in, var_in, frames)
    mix = jnp.stack([mix_real[:, :, :count], mix_imag[:, :, :count]])
    peers = lax.axis_size("frame")
    bins = mix.shape[2]
    mix = frame_gather(mix.reshape(-1, 128), peers)
    mix = mix.reshape(peers, 2, count, bins, count).transpose(1, 2, 0, 3, 4)
    mix = mix.reshape(2, count, peers * bins, count)
    mix_real, mix_imag = mix[0], mix[1]
    top = jnp.concatenate([mix_real, -mix_imag], axis=2)
    bottom = jnp.concatenate([mix_imag, mix_real], axis=2)
    mix = jnp.concatenate([top, bottom], axis=0)
    stacked = spectra.reshape(2 * count, spectra.shape[2], spectra.shape[3]).astype(jnp.float32)
    demixed = jnp.einsum(
        "jfa,aft->jft", mix, stacked, precision=lax.Precision.HIGHEST,
        preferred_element_type=jnp.float32,
    )
    return (demixed.reshape(spectra.shape), variances)


def solution(mesh):
    in_specs = (P(None, None, "freq", "frame"), P(), P(), P(), P(), P(), P(), P())
    out_specs = (P(None, None, "freq", "frame"), P(None, "freq", "frame"))
    return jax.shard_map(
        on_device, mesh=mesh, in_specs=in_specs, out_specs=out_specs, check_vma=False
    )
```

```python
import functools

import jax
import jax.numpy as jnp
from jax import lax
from jax.experimental import pallas as pl
from jax.experimental.pallas import tpu as pltpu
from jax.sharding import PartitionSpec as P

epsilon = 1e-05
power_floor = 0.001
variance_floor = 0.25


def source_model(spectra, norm_gain, w_in, b_in, w_mid, b_mid, w_out, b_out):
    real_part = spectra[0].astype(jnp.float32)
    imag_part = spectra[1].astype(jnp.float32)
    logpower = jnp.log(real_part * real_part + imag_part * imag_part + power_floor).astype(
        jnp.bfloat16
    )
    count, freq, span = logpower.shape
    shards = lax.axis_size("freq")
    rows = span // shards
    send = logpower.transpose(0, 2, 1).reshape(count, shards, rows, freq).transpose(1, 0, 2, 3)
    received = lax.all_to_all(send, "freq", split_axis=0, concat_axis=0, tiled=True)
    values = received.transpose(1, 2, 0, 3).reshape(count, rows, shards * freq).astype(jnp.float32)
    average = jnp.mean(values, axis=2, keepdims=True)
    centred = values - average
    spread = jnp.mean(centred * centred, axis=2, keepdims=True)
    normed = (centred * lax.rsqrt(spread + epsilon) * norm_gain).astype(jnp.bfloat16)
    hidden_one = jax.nn.silu(
        jnp.einsum("ntf,fh->nth", normed, w_in, preferred_element_type=jnp.float32) + b_in
    ).astype(jnp.bfloat16)
    hidden_two = jax.nn.silu(
        jnp.einsum("nth,hg->ntg", hidden_one, w_mid, preferred_element_type=jnp.float32) + b_mid
    ).astype(jnp.bfloat16)
    output_pre = (
        jnp.einsum("nth,hf->ntf", hidden_two, w_out, preferred_element_type=jnp.float32) + b_out
    )
    frame_variances = (jax.nn.softplus(output_pre) + variance_floor).astype(jnp.bfloat16)
    send = frame_variances.reshape(count, rows, shards, freq).transpose(2, 0, 1, 3)
    received = lax.all_to_all(send, "freq", split_axis=0, concat_axis=0, tiled=True)
    return received.transpose(1, 3, 0, 2).reshape(count, freq, span), received


def sweep_kernel(frames, spec_in, var_in, mr_ref, mi_ref, yr, yi, w, pr, pi, pp):
    count, bins, length = yr.shape
    peers, _, _, span = spec_in.shape
    chunk = 512
    chunks = length // chunk

    def init(s, carry):
        cols = pl.ds(pl.multiple_of(s * span, span), span)

        def per_pair(p, carry):
            block = var_in[s, p].astype(jnp.float32)
            w[2 * p, :, cols] = 1.0 / block[:bins]
            w[2 * p + 1, :, cols] = 1.0 / block[bins:]
            for half in range(2):
                j = 2 * p + half
                spec = spec_in[s, j].astype(jnp.float32)
                yr[j, :, cols] = spec[:bins]
                yi[j, :, cols] = spec[bins:]
            return carry

        lax.fori_loop(0, count // 2, per_pair, 0)
        return carry

    lax.fori_loop(0, peers, init, 0)

    def init_mix(j, carry):
        lane = lax.broadcasted_iota(jnp.int32, (bins, mr_ref.shape[2]), 1)
        mr_ref[j] = jnp.where(lane == j, 1.0, 0.0).astype(jnp.float32)
        mi_ref[j] = jnp.zeros((bins, mr_ref.shape[2]), jnp.float32)
        return carry

    lax.fori_loop(0, count, init_mix, 0)

    def step(k, carry):
        pr[...] = yr[k]
        pi[...] = yi[k]
        pp[...] = pr[...] * pr[...] + pi[...] * pi[...]
        mkr = mr_ref[k]
        mki = mi_ref[k]

        def per_source(j, carry):
            acc_r = jnp.zeros((bins, chunk), jnp.float32)
            acc_i = jnp.zeros((bins, chunk), jnp.float32)
            acc_d = jnp.zeros((bins, chunk), jnp.float32)
            for c in range(chunks):
                sl = pl.ds(c * chunk, chunk)
                a_r = yr[j, :, sl]
                a_i = yi[j, :, sl]
                ww = w[j, :, sl]
                b_r = pr[:, sl]
                b_i = pi[:, sl]
                acc_r = acc_r + ww * (a_r * b_r + a_i * b_i)
                acc_i = acc_i + ww * (a_i * b_r - a_r * b_i)
                acc_d = acc_d + ww * pp[:, sl]
            numer_real = jnp.sum(acc_r, axis=1, keepdims=True) / frames
            numer_imag = jnp.sum(acc_i, axis=1, keepdims=True) / frames
            denom = jnp.sum(acc_d, axis=1, keepdims=True) / frames
            is_self = j == k
            coef_real = jnp.where(is_self, 1.0 - lax.rsqrt(denom), numer_real / denom)
            coef_imag = jnp.where(is_self, 0.0, numer_imag / denom)
            for c in range(chunks):
                sl = pl.ds(c * chunk, chunk)
                b_r = pr[:, sl]
                b_i = pi[:, sl]
                yr[j, :, sl] = yr[j, :, sl] - (coef_real * b_r - coef_imag * b_i)
                yi[j, :, sl] = yi[j, :, sl] - (coef_real * b_i + coef_imag * b_r)
            mr_ref[j] = mr_ref[j] - (coef_real * mkr - coef_imag * mki)
            mi_ref[j] = mi_ref[j] - (coef_real * mki + coef_imag * mkr)
            return carry

        lax.fori_loop(0, count, per_source, 0)
        return carry

    lax.fori_loop(0, count, step, 0)


def sweep(spec_in, var_in, frames):
    _, count, rows, _ = spec_in.shape
    bins, length = rows // 2, frames
    lanes = 128
    vmem = pl.BlockSpec(memory_space=pltpu.VMEM)
    return pl.pallas_call(
        functools.partial(sweep_kernel, frames),
        out_shape=(
            jax.ShapeDtypeStruct((count, bins, lanes), jnp.float32),
            jax.ShapeDtypeStruct((count, bins, lanes), jnp.float32),
        ),
        in_specs=[vmem, vmem],
        out_specs=(vmem, vmem),
        scratch_shapes=[
            pltpu.VMEM((count, bins, length), jnp.float32),
            pltpu.VMEM((count, bins, length), jnp.float32),
            pltpu.VMEM((count, bins, length), jnp.float32),
            pltpu.VMEM((bins, length), jnp.float32),
            pltpu.VMEM((bins, length), jnp.float32),
            pltpu.VMEM((bins, length), jnp.float32),
        ],
        compiler_params=pltpu.CompilerParams(vmem_limit_bytes=60 * 1024 * 1024),
    )(spec_in, var_in)


def gather_kernel(x_ref, o_ref, send_sem, recv_sem, local_sem):
    n = o_ref.shape[0]
    me = lax.axis_index("frame")
    fq = lax.axis_index("freq")
    barrier = pltpu.get_barrier_semaphore()
    for d in range(1, n):
        peer = lax.rem(me + d, n)
        pl.semaphore_signal(barrier, inc=1, device_id=(fq, peer), device_id_type=pl.DeviceIdType.MESH)
    pl.semaphore_wait(barrier, n - 1)
    local = pltpu.make_async_copy(x_ref, o_ref.at[me], local_sem)
    local.start()
    copies = []
    for d in range(1, n):
        peer = lax.rem(me + d, n)
        copy = pltpu.make_async_remote_copy(
            src_ref=x_ref, dst_ref=o_ref.at[me], send_sem=send_sem.at[d], recv_sem=recv_sem.at[d],
            device_id=(fq, peer), device_id_type=pl.DeviceIdType.MESH,
        )
        copy.start()
        copies.append(copy)
    for d in range(1, n):
        source = lax.rem(me + n - d, n)
        copies[d - 1].wait_send()
        incoming = pltpu.make_async_remote_copy(
            src_ref=x_ref, dst_ref=o_ref.at[source], send_sem=send_sem.at[d], recv_sem=recv_sem.at[d],
            device_id=(fq, source), device_id_type=pl.DeviceIdType.MESH,
        )
        incoming.wait_recv()
    local.wait()


def frame_gather(x, n):
    vmem = pl.BlockSpec(memory_space=pltpu.VMEM)
    return pl.pallas_call(
        gather_kernel,
        out_shape=jax.ShapeDtypeStruct((n,) + x.shape, x.dtype),
        in_specs=[vmem],
        out_specs=vmem,
        scratch_shapes=[
            pltpu.SemaphoreType.DMA((n,)),
            pltpu.SemaphoreType.DMA((n,)),
            pltpu.SemaphoreType.DMA,
        ],
        compiler_params=pltpu.CompilerParams(collective_id=0, has_side_effects=True),
    )(x)


def on_device(spectra, norm_gain, w_in, b_in, w_mid, b_mid, w_out, b_out):
    count = spectra.shape[1]
    frames = spectra.shape[3] * lax.axis_size("frame")
    variances, received = source_model(spectra, norm_gain, w_in, b_in, w_mid, b_mid, w_out, b_out)

    peers = lax.axis_size("frame")
    _, _, freq, span = spectra.shape
    bins = freq // peers
    spec_send = spectra.reshape(2, count, peers, bins, span).transpose(2, 1, 0, 3, 4)
    spec_send = spec_send.reshape(peers, count, 2 * bins, span)
    shards, rows = received.shape[0], received.shape[2]
    var_send = received.reshape(shards, count // 2, 2, rows, peers, bins)
    var_send = var_send.transpose(4, 1, 2, 5, 0, 3).reshape(peers, count // 2, 2 * bins, span)
    spec_in = lax.all_to_all(spec_send, "frame", split_axis=0, concat_axis=0, tiled=True)
    var_in = lax.all_to_all(var_send, "frame", split_axis=0, concat_axis=0, tiled=True)
    mix_real, mix_imag = sweep(spec_in, var_in, frames)
    mix = jnp.stack([mix_real[:, :, :count], mix_imag[:, :, :count]])
    peers = lax.axis_size("frame")
    bins = mix.shape[2]
    mix = frame_gather(mix.reshape(-1, 128), peers)
    mix = mix.reshape(peers, 2, count, bins, count).transpose(1, 2, 0, 3, 4)
    mix = mix.reshape(2, count, peers * bins, count)
    mix_real, mix_imag = mix[0], mix[1]
    top = jnp.concatenate([mix_real, -mix_imag], axis=2)
    bottom = jnp.concatenate([mix_imag, mix_real], axis=2)
    mix = jnp.concatenate([top, bottom], axis=0)
    stacked = spectra.reshape(2 * count, spectra.shape[2], spectra.shape[3]).astype(jnp.float32)
    demixed = jnp.einsum(
        "jfa,aft->jft", mix, stacked, precision=lax.Precision.HIGHEST,
        preferred_element_type=jnp.float32,
    )
    return (demixed.reshape(spectra.shape), variances)


def solution(mesh):
    in_specs = (P(None, None, "freq", "frame"), P(), P(), P(), P(), P(), P(), P())
    out_specs = (P(None, None, "freq", "frame"), P(None, "freq", "frame"))
    return jax.shard_map(
        on_device, mesh=mesh, in_specs=in_specs, out_specs=out_specs, check_vma=False
    )
```

```python
import functools

import jax
import jax.numpy as jnp
from jax import lax
from jax.experimental import pallas as pl
from jax.experimental.pallas import tpu as pltpu
from jax.sharding import PartitionSpec as P

epsilon = 1e-05
power_floor = 0.001
variance_floor = 0.25


def source_model(spectra, norm_gain, w_in, b_in, w_mid, b_mid, w_out, b_out):
    real_part = spectra[0].astype(jnp.float32)
    imag_part = spectra[1].astype(jnp.float32)
    logpower = jnp.log(real_part * real_part + imag_part * imag_part + power_floor).astype(
        jnp.bfloat16
    )
    count, freq, span = logpower.shape
    shards = lax.axis_size("freq")
    rows = span // shards
    send = logpower.transpose(0, 2, 1).reshape(count, shards, rows, freq).transpose(1, 0, 2, 3)
    received = lax.all_to_all(send, "freq", split_axis=0, concat_axis=0, tiled=True)
    values = received.transpose(1, 2, 0, 3).reshape(count, rows, shards * freq).astype(jnp.float32)
    average = jnp.mean(values, axis=2, keepdims=True)
    centred = values - average
    spread = jnp.mean(centred * centred, axis=2, keepdims=True)
    normed = (centred * lax.rsqrt(spread + epsilon) * norm_gain).astype(jnp.bfloat16)
    hidden_one = jax.nn.silu(
        jnp.einsum("ntf,fh->nth", normed, w_in, preferred_element_type=jnp.float32) + b_in
    ).astype(jnp.bfloat16)
    hidden_two = jax.nn.silu(
        jnp.einsum("nth,hg->ntg", hidden_one, w_mid, preferred_element_type=jnp.float32) + b_mid
    ).astype(jnp.bfloat16)
    output_pre = (
        jnp.einsum("nth,hf->ntf", hidden_two, w_out, preferred_element_type=jnp.float32) + b_out
    )
    frame_variances = (jax.nn.softplus(output_pre) + variance_floor).astype(jnp.bfloat16)
    send = frame_variances.reshape(count, rows, shards, freq).transpose(2, 0, 1, 3)
    received = lax.all_to_all(send, "freq", split_axis=0, concat_axis=0, tiled=True)
    return received.transpose(1, 3, 0, 2).reshape(count, freq, span)


def sweep_kernel(frames, spec_in, var_in, mr_ref, mi_ref, yr, yi, w, pr, pi, pp):
    count, bins, length = yr.shape
    peers, _, _, span = spec_in.shape
    chunk = 512
    chunks = length // chunk

    def init(s, carry):
        cols = pl.ds(pl.multiple_of(s * span, span), span)

        def per_pair(p, carry):
            block = var_in[s, p].astype(jnp.float32)
            w[2 * p, :, cols] = 1.0 / block[:bins]
            w[2 * p + 1, :, cols] = 1.0 / block[bins:]
            for half in range(2):
                j = 2 * p + half
                spec = spec_in[s, j].astype(jnp.float32)
                yr[j, :, cols] = spec[:bins]
                yi[j, :, cols] = spec[bins:]
            return carry

        lax.fori_loop(0, count // 2, per_pair, 0)
        return carry

    lax.fori_loop(0, peers, init, 0)

    def init_mix(j, carry):
        lane = lax.broadcasted_iota(jnp.int32, (bins, mr_ref.shape[2]), 1)
        mr_ref[j] = jnp.where(lane == j, 1.0, 0.0).astype(jnp.float32)
        mi_ref[j] = jnp.zeros((bins, mr_ref.shape[2]), jnp.float32)
        return carry

    lax.fori_loop(0, count, init_mix, 0)

    def step(k, carry):
        pr[...] = yr[k]
        pi[...] = yi[k]
        pp[...] = pr[...] * pr[...] + pi[...] * pi[...]
        mkr = mr_ref[k]
        mki = mi_ref[k]

        def per_source(j, carry):
            acc_r = jnp.zeros((bins, chunk), jnp.float32)
            acc_i = jnp.zeros((bins, chunk), jnp.float32)
            acc_d = jnp.zeros((bins, chunk), jnp.float32)
            for c in range(chunks):
                sl = pl.ds(c * chunk, chunk)
                a_r = yr[j, :, sl]
                a_i = yi[j, :, sl]
                ww = w[j, :, sl]
                b_r = pr[:, sl]
                b_i = pi[:, sl]
                acc_r = acc_r + ww * (a_r * b_r + a_i * b_i)
                acc_i = acc_i + ww * (a_i * b_r - a_r * b_i)
                acc_d = acc_d + ww * pp[:, sl]
            numer_real = jnp.sum(acc_r, axis=1, keepdims=True) / frames
            numer_imag = jnp.sum(acc_i, axis=1, keepdims=True) / frames
            denom = jnp.sum(acc_d, axis=1, keepdims=True) / frames
            is_self = j == k
            coef_real = jnp.where(is_self, 1.0 - lax.rsqrt(denom), numer_real / denom)
            coef_imag = jnp.where(is_self, 0.0, numer_imag / denom)
            for c in range(chunks):
                sl = pl.ds(c * chunk, chunk)
                b_r = pr[:, sl]
                b_i = pi[:, sl]
                yr[j, :, sl] = yr[j, :, sl] - (coef_real * b_r - coef_imag * b_i)
                yi[j, :, sl] = yi[j, :, sl] - (coef_real * b_i + coef_imag * b_r)
            mr_ref[j] = mr_ref[j] - (coef_real * mkr - coef_imag * mki)
            mi_ref[j] = mi_ref[j] - (coef_real * mki + coef_imag * mkr)
            return carry

        lax.fori_loop(0, count, per_source, 0)
        return carry

    lax.fori_loop(0, count, step, 0)


def sweep(spec_in, var_in, frames):
    _, count, rows, _ = spec_in.shape
    bins, length = rows // 2, frames
    lanes = 128
    vmem = pl.BlockSpec(memory_space=pltpu.VMEM)
    return pl.pallas_call(
        functools.partial(sweep_kernel, frames),
        out_shape=(
            jax.ShapeDtypeStruct((count, bins, lanes), jnp.float32),
            jax.ShapeDtypeStruct((count, bins, lanes), jnp.float32),
        ),
        in_specs=[vmem, vmem],
        out_specs=(vmem, vmem),
        scratch_shapes=[
            pltpu.VMEM((count, bins, length), jnp.float32),
            pltpu.VMEM((count, bins, length), jnp.float32),
            pltpu.VMEM((count, bins, length), jnp.float32),
            pltpu.VMEM((bins, length), jnp.float32),
            pltpu.VMEM((bins, length), jnp.float32),
            pltpu.VMEM((bins, length), jnp.float32),
        ],
        compiler_params=pltpu.CompilerParams(vmem_limit_bytes=60 * 1024 * 1024),
    )(spec_in, var_in)


def gather_kernel(x_ref, o_ref, send_sem, recv_sem, local_sem):
    n = o_ref.shape[0]
    me = lax.axis_index("frame")
    fq = lax.axis_index("freq")
    barrier = pltpu.get_barrier_semaphore()
    for d in range(1, n):
        peer = lax.rem(me + d, n)
        pl.semaphore_signal(barrier, inc=1, device_id=(fq, peer), device_id_type=pl.DeviceIdType.MESH)
    pl.semaphore_wait(barrier, n - 1)
    local = pltpu.make_async_copy(x_ref, o_ref.at[me], local_sem)
    local.start()
    copies = []
    for d in range(1, n):
        peer = lax.rem(me + d, n)
        copy = pltpu.make_async_remote_copy(
            src_ref=x_ref, dst_ref=o_ref.at[me], send_sem=send_sem.at[d], recv_sem=recv_sem.at[d],
            device_id=(fq, peer), device_id_type=pl.DeviceIdType.MESH,
        )
        copy.start()
        copies.append(copy)
    for d in range(1, n):
        source = lax.rem(me + n - d, n)
        copies[d - 1].wait_send()
        incoming = pltpu.make_async_remote_copy(
            src_ref=x_ref, dst_ref=o_ref.at[source], send_sem=send_sem.at[d], recv_sem=recv_sem.at[d],
            device_id=(fq, source), device_id_type=pl.DeviceIdType.MESH,
        )
        incoming.wait_recv()
    local.wait()


def frame_gather(x, n):
    vmem = pl.BlockSpec(memory_space=pltpu.VMEM)
    return pl.pallas_call(
        gather_kernel,
        out_shape=jax.ShapeDtypeStruct((n,) + x.shape, x.dtype),
        in_specs=[vmem],
        out_specs=vmem,
        scratch_shapes=[
            pltpu.SemaphoreType.DMA((n,)),
            pltpu.SemaphoreType.DMA((n,)),
            pltpu.SemaphoreType.DMA,
        ],
        compiler_params=pltpu.CompilerParams(collective_id=0, has_side_effects=True),
    )(x)


def on_device(spectra, norm_gain, w_in, b_in, w_mid, b_mid, w_out, b_out):
    count = spectra.shape[1]
    frames = spectra.shape[3] * lax.axis_size("frame")
    variances = source_model(spectra, norm_gain, w_in, b_in, w_mid, b_mid, w_out, b_out)

    peers = lax.axis_size("frame")
    _, _, freq, span = spectra.shape
    bins = freq // peers
    spec_send = spectra.reshape(2, count, peers, bins, span).transpose(2, 1, 0, 3, 4)
    spec_send = spec_send.reshape(peers, count, 2 * bins, span)
    var_send = variances.reshape(count // 2, 2, peers, bins, span).transpose(2, 0, 1, 3, 4)
    var_send = var_send.reshape(peers, count // 2, 2 * bins, span)
    spec_in = lax.all_to_all(spec_send, "frame", split_axis=0, concat_axis=0, tiled=True)
    var_in = lax.all_to_all(var_send, "frame", split_axis=0, concat_axis=0, tiled=True)
    mix_real, mix_imag = sweep(spec_in, var_in, frames)
    mix = jnp.stack([mix_real[:, :, :count], mix_imag[:, :, :count]])
    peers = lax.axis_size("frame")
    bins = mix.shape[2]
    mix = frame_gather(mix.reshape(-1, 128), peers)
    mix = mix.reshape(peers, 2, count, bins, count).transpose(1, 2, 0, 3, 4)
    mix = mix.reshape(2, count, peers * bins, count)
    mix_real, mix_imag = mix[0], mix[1]
    top = jnp.concatenate([mix_real, -mix_imag], axis=2)
    bottom = jnp.concatenate([mix_imag, mix_real], axis=2)
    mix = jnp.concatenate([top, bottom], axis=0)
    stacked = spectra.reshape(2 * count, spectra.shape[2], spectra.shape[3]).astype(jnp.float32)
    demixed = jnp.einsum(
        "jfa,aft->jft", mix, stacked, precision=lax.Precision.HIGH,
        preferred_element_type=jnp.float32,
    )
    return (demixed.reshape(spectra.shape), variances)


def solution(mesh):
    in_specs = (P(None, None, "freq", "frame"), P(), P(), P(), P(), P(), P(), P())
    out_specs = (P(None, None, "freq", "frame"), P(None, "freq", "frame"))
    return jax.shard_map(
        on_device, mesh=mesh, in_specs=in_specs, out_specs=out_specs, check_vma=False
    )
```

```python
import functools

import jax
import jax.numpy as jnp
from jax import lax
from jax.experimental import pallas as pl
from jax.experimental.pallas import tpu as pltpu
from jax.sharding import PartitionSpec as P

epsilon = 1e-05
power_floor = 0.001
variance_floor = 0.25


def source_model(spectra, norm_gain, w_in, b_in, w_mid, b_mid, w_out, b_out):
    real_part = spectra[0].astype(jnp.float32)
    imag_part = spectra[1].astype(jnp.float32)
    logpower = jnp.log(real_part * real_part + imag_part * imag_part + power_floor).astype(
        jnp.bfloat16
    )
    count, freq, span = logpower.shape
    shards = lax.axis_size("freq")
    rows = span // shards
    send = logpower.transpose(0, 2, 1).reshape(count, shards, rows, freq).transpose(1, 0, 2, 3)
    received = lax.all_to_all(send, "freq", split_axis=0, concat_axis=0, tiled=True)
    values = received.transpose(1, 2, 0, 3).reshape(count, rows, shards * freq).astype(jnp.float32)
    average = jnp.mean(values, axis=2, keepdims=True)
    centred = values - average
    spread = jnp.mean(centred * centred, axis=2, keepdims=True)
    normed = (centred * lax.rsqrt(spread + epsilon) * norm_gain).astype(jnp.bfloat16)
    hidden_one = jax.nn.silu(
        jnp.einsum("ntf,fh->nth", normed, w_in, preferred_element_type=jnp.float32) + b_in
    ).astype(jnp.bfloat16)
    hidden_two = jax.nn.silu(
        jnp.einsum("nth,hg->ntg", hidden_one, w_mid, preferred_element_type=jnp.float32) + b_mid
    ).astype(jnp.bfloat16)
    output_pre = (
        jnp.einsum("nth,hf->ntf", hidden_two, w_out, preferred_element_type=jnp.float32) + b_out
    )
    frame_variances = (jax.nn.softplus(output_pre) + variance_floor).astype(jnp.bfloat16)
    send = frame_variances.reshape(count, rows, shards, freq).transpose(2, 0, 1, 3)
    received = lax.all_to_all(send, "freq", split_axis=0, concat_axis=0, tiled=True)
    return received.transpose(1, 3, 0, 2).reshape(count, freq, span)


def sweep_kernel(frames, spec_in, var_in, mr_ref, mi_ref, yr, yi, w, pr, pi, pp):
    count, bins, length = yr.shape
    peers, _, _, span = spec_in.shape
    chunk = 256
    chunks = length // chunk

    def init(s, carry):
        cols = pl.ds(pl.multiple_of(s * span, span), span)

        def per_pair(p, carry):
            block = var_in[s, p].astype(jnp.float32)
            w[2 * p, :, cols] = 1.0 / block[:bins]
            w[2 * p + 1, :, cols] = 1.0 / block[bins:]
            for half in range(2):
                j = 2 * p + half
                spec = spec_in[s, j].astype(jnp.float32)
                yr[j, :, cols] = spec[:bins]
                yi[j, :, cols] = spec[bins:]
            return carry

        lax.fori_loop(0, count // 2, per_pair, 0)
        return carry

    lax.fori_loop(0, peers, init, 0)

    def init_mix(j, carry):
        lane = lax.broadcasted_iota(jnp.int32, (bins, mr_ref.shape[2]), 1)
        mr_ref[j] = jnp.where(lane == j, 1.0, 0.0).astype(jnp.float32)
        mi_ref[j] = jnp.zeros((bins, mr_ref.shape[2]), jnp.float32)
        return carry

    lax.fori_loop(0, count, init_mix, 0)

    def step(k, carry):
        pr[...] = yr[k]
        pi[...] = yi[k]
        pp[...] = pr[...] * pr[...] + pi[...] * pi[...]
        mkr = mr_ref[k]
        mki = mi_ref[k]

        def per_pair(p, carry):
            sources = tuple(4 * p + h for h in range(4))
            acc = [[jnp.zeros((bins, chunk), jnp.float32) for _ in range(3)] for _ in sources]
            for c in range(chunks):
                sl = pl.ds(c * chunk, chunk)
                b_r = pr[:, sl]
                b_i = pi[:, sl]
                b_p = pp[:, sl]
                for h, j in enumerate(sources):
                    a_r = yr[j, :, sl]
                    a_i = yi[j, :, sl]
                    ww = w[j, :, sl]
                    acc[h][0] = acc[h][0] + ww * (a_r * b_r + a_i * b_i)
                    acc[h][1] = acc[h][1] + ww * (a_i * b_r - a_r * b_i)
                    acc[h][2] = acc[h][2] + ww * b_p
            coefs = []
            for h, j in enumerate(sources):
                numer_real = jnp.sum(acc[h][0], axis=1, keepdims=True) / frames
                numer_imag = jnp.sum(acc[h][1], axis=1, keepdims=True) / frames
                denom = jnp.sum(acc[h][2], axis=1, keepdims=True) / frames
                is_self = j == k
                coef_real = jnp.where(is_self, 1.0 - lax.rsqrt(denom), numer_real / denom)
                coef_imag = jnp.where(is_self, 0.0, numer_imag / denom)
                coefs.append((coef_real, coef_imag))
            for c in range(chunks):
                sl = pl.ds(c * chunk, chunk)
                b_r = pr[:, sl]
                b_i = pi[:, sl]
                for j, (coef_real, coef_imag) in zip(sources, coefs):
                    yr[j, :, sl] = yr[j, :, sl] - (coef_real * b_r - coef_imag * b_i)
                    yi[j, :, sl] = yi[j, :, sl] - (coef_real * b_i + coef_imag * b_r)
            for j, (coef_real, coef_imag) in zip(sources, coefs):
                mr_ref[j] = mr_ref[j] - (coef_real * mkr - coef_imag * mki)
                mi_ref[j] = mi_ref[j] - (coef_real * mki + coef_imag * mkr)
            return carry

        lax.fori_loop(0, count // 4, per_pair, 0)
        return carry

    lax.fori_loop(0, count, step, 0)


def sweep(spec_in, var_in, frames):
    _, count, rows, _ = spec_in.shape
    bins, length = rows // 2, frames
    lanes = 128
    vmem = pl.BlockSpec(memory_space=pltpu.VMEM)
    return pl.pallas_call(
        functools.partial(sweep_kernel, frames),
        out_shape=(
            jax.ShapeDtypeStruct((count, bins, lanes), jnp.float32),
            jax.ShapeDtypeStruct((count, bins, lanes), jnp.float32),
        ),
        in_specs=[vmem, vmem],
        out_specs=(vmem, vmem),
        scratch_shapes=[
            pltpu.VMEM((count, bins, length), jnp.float32),
            pltpu.VMEM((count, bins, length), jnp.float32),
            pltpu.VMEM((count, bins, length), jnp.float32),
            pltpu.VMEM((bins, length), jnp.float32),
            pltpu.VMEM((bins, length), jnp.float32),
            pltpu.VMEM((bins, length), jnp.float32),
        ],
        compiler_params=pltpu.CompilerParams(vmem_limit_bytes=60 * 1024 * 1024),
    )(spec_in, var_in)


def gather_kernel(x_ref, o_ref, send_sem, recv_sem, local_sem):
    n = o_ref.shape[0]
    me = lax.axis_index("frame")
    fq = lax.axis_index("freq")
    barrier = pltpu.get_barrier_semaphore()
    for d in range(1, n):
        peer = lax.rem(me + d, n)
        pl.semaphore_signal(barrier, inc=1, device_id=(fq, peer), device_id_type=pl.DeviceIdType.MESH)
    pl.semaphore_wait(barrier, n - 1)
    local = pltpu.make_async_copy(x_ref, o_ref.at[me], local_sem)
    local.start()
    copies = []
    for d in range(1, n):
        peer = lax.rem(me + d, n)
        copy = pltpu.make_async_remote_copy(
            src_ref=x_ref, dst_ref=o_ref.at[me], send_sem=send_sem.at[d], recv_sem=recv_sem.at[d],
            device_id=(fq, peer), device_id_type=pl.DeviceIdType.MESH,
        )
        copy.start()
        copies.append(copy)
    for d in range(1, n):
        source = lax.rem(me + n - d, n)
        copies[d - 1].wait_send()
        incoming = pltpu.make_async_remote_copy(
            src_ref=x_ref, dst_ref=o_ref.at[source], send_sem=send_sem.at[d], recv_sem=recv_sem.at[d],
            device_id=(fq, source), device_id_type=pl.DeviceIdType.MESH,
        )
        incoming.wait_recv()
    local.wait()


def frame_gather(x, n):
    vmem = pl.BlockSpec(memory_space=pltpu.VMEM)
    return pl.pallas_call(
        gather_kernel,
        out_shape=jax.ShapeDtypeStruct((n,) + x.shape, x.dtype),
        in_specs=[vmem],
        out_specs=vmem,
        scratch_shapes=[
            pltpu.SemaphoreType.DMA((n,)),
            pltpu.SemaphoreType.DMA((n,)),
            pltpu.SemaphoreType.DMA,
        ],
        compiler_params=pltpu.CompilerParams(collective_id=0, has_side_effects=True),
    )(x)


def on_device(spectra, norm_gain, w_in, b_in, w_mid, b_mid, w_out, b_out):
    count = spectra.shape[1]
    frames = spectra.shape[3] * lax.axis_size("frame")
    variances = source_model(spectra, norm_gain, w_in, b_in, w_mid, b_mid, w_out, b_out)

    peers = lax.axis_size("frame")
    _, _, freq, span = spectra.shape
    bins = freq // peers
    spec_send = spectra.reshape(2, count, peers, bins, span).transpose(2, 1, 0, 3, 4)
    spec_send = spec_send.reshape(peers, count, 2 * bins, span)
    var_send = variances.reshape(count // 2, 2, peers, bins, span).transpose(2, 0, 1, 3, 4)
    var_send = var_send.reshape(peers, count // 2, 2 * bins, span)
    spec_in = lax.all_to_all(spec_send, "frame", split_axis=0, concat_axis=0, tiled=True)
    var_in = lax.all_to_all(var_send, "frame", split_axis=0, concat_axis=0, tiled=True)
    mix_real, mix_imag = sweep(spec_in, var_in, frames)
    mix = jnp.stack([mix_real[:, :, :count], mix_imag[:, :, :count]])
    peers = lax.axis_size("frame")
    bins = mix.shape[2]
    mix = frame_gather(mix.reshape(-1, 128), peers)
    mix = mix.reshape(peers, 2, count, bins, count).transpose(1, 2, 0, 3, 4)
    mix = mix.reshape(2, count, peers * bins, count)
    mix_real, mix_imag = mix[0], mix[1]
    top = jnp.concatenate([mix_real, -mix_imag], axis=2)
    bottom = jnp.concatenate([mix_imag, mix_real], axis=2)
    mix = jnp.concatenate([top, bottom], axis=0)
    stacked = spectra.reshape(2 * count, spectra.shape[2], spectra.shape[3]).astype(jnp.float32)
    demixed = jnp.einsum(
        "jfa,aft->jft", mix, stacked, precision=lax.Precision.HIGH,
        preferred_element_type=jnp.float32,
    )
    return (demixed.reshape(spectra.shape), variances)


def solution(mesh):
    in_specs = (P(None, None, "freq", "frame"), P(), P(), P(), P(), P(), P(), P())
    out_specs = (P(None, None, "freq", "frame"), P(None, "freq", "frame"))
    return jax.shard_map(
        on_device, mesh=mesh, in_specs=in_specs, out_specs=out_specs, check_vma=False
    )
```

```python
import functools

import jax
import jax.numpy as jnp
from jax import lax
from jax.experimental import pallas as pl
from jax.experimental.pallas import tpu as pltpu
from jax.sharding import PartitionSpec as P

epsilon = 1e-05
power_floor = 0.001
variance_floor = 0.25


def source_model(spectra, norm_gain, w_in, b_in, w_mid, b_mid, w_out, b_out):
    real_part = spectra[0].astype(jnp.float32)
    imag_part = spectra[1].astype(jnp.float32)
    logpower = jnp.log(real_part * real_part + imag_part * imag_part + power_floor).astype(
        jnp.bfloat16
    )
    count, freq, span = logpower.shape
    shards = lax.axis_size("freq")
    rows = span // shards
    send = logpower.transpose(0, 2, 1).reshape(count, shards, rows, freq).transpose(1, 0, 2, 3)
    received = lax.all_to_all(send, "freq", split_axis=0, concat_axis=0, tiled=True)
    values = received.transpose(1, 2, 0, 3).reshape(count, rows, shards * freq).astype(jnp.float32)
    average = jnp.mean(values, axis=2, keepdims=True)
    centred = values - average
    spread = jnp.mean(centred * centred, axis=2, keepdims=True)
    normed = (centred * lax.rsqrt(spread + epsilon) * norm_gain).astype(jnp.bfloat16)
    hidden_one = jax.nn.silu(
        jnp.einsum("ntf,fh->nth", normed, w_in, preferred_element_type=jnp.float32) + b_in
    ).astype(jnp.bfloat16)
    hidden_two = jax.nn.silu(
        jnp.einsum("nth,hg->ntg", hidden_one, w_mid, preferred_element_type=jnp.float32) + b_mid
    ).astype(jnp.bfloat16)
    output_pre = (
        jnp.einsum("nth,hf->ntf", hidden_two, w_out, preferred_element_type=jnp.float32) + b_out
    )
    frame_variances = (jax.nn.softplus(output_pre) + variance_floor).astype(jnp.bfloat16)
    send = frame_variances.reshape(count, rows, shards, freq).transpose(2, 0, 1, 3)
    received = lax.all_to_all(send, "freq", split_axis=0, concat_axis=0, tiled=True)
    return received.transpose(1, 3, 0, 2).reshape(count, freq, span)


def sweep_kernel(frames, spec_in, var_in, mr_ref, mi_ref, yr, yi, w, pr, pi, pp):
    count, bins, length = yr.shape
    peers, _, _, span = spec_in.shape
    chunk = 256
    chunks = length // chunk

    def init(s, carry):
        cols = pl.ds(pl.multiple_of(s * span, span), span)

        def per_pair(p, carry):
            block = var_in[s, p].astype(jnp.float32)
            w[2 * p, :, cols] = 1.0 / block[:bins]
            w[2 * p + 1, :, cols] = 1.0 / block[bins:]
            for half in range(2):
                j = 2 * p + half
                spec = spec_in[s, j].astype(jnp.float32)
                yr[j, :, cols] = spec[:bins]
                yi[j, :, cols] = spec[bins:]
            return carry

        lax.fori_loop(0, count // 2, per_pair, 0)
        return carry

    lax.fori_loop(0, peers, init, 0)

    def init_mix(j, carry):
        lane = lax.broadcasted_iota(jnp.int32, (bins, mr_ref.shape[2]), 1)
        mr_ref[j] = jnp.where(lane == j, 1.0, 0.0).astype(jnp.float32)
        mi_ref[j] = jnp.zeros((bins, mr_ref.shape[2]), jnp.float32)
        return carry

    lax.fori_loop(0, count, init_mix, 0)

    def step(k, carry):
        pr[...] = yr[k]
        pi[...] = yi[k]
        pp[...] = pr[...] * pr[...] + pi[...] * pi[...]
        mkr = mr_ref[k]
        mki = mi_ref[k]

        def per_pair(p, carry):
            sources = tuple(6 * p + h for h in range(6))
            acc = [[jnp.zeros((bins, chunk), jnp.float32) for _ in range(3)] for _ in sources]
            for c in range(chunks):
                sl = pl.ds(c * chunk, chunk)
                b_r = pr[:, sl]
                b_i = pi[:, sl]
                b_p = pp[:, sl]
                for h, j in enumerate(sources):
                    a_r = yr[j, :, sl]
                    a_i = yi[j, :, sl]
                    ww = w[j, :, sl]
                    acc[h][0] = acc[h][0] + ww * (a_r * b_r + a_i * b_i)
                    acc[h][1] = acc[h][1] + ww * (a_i * b_r - a_r * b_i)
                    acc[h][2] = acc[h][2] + ww * b_p
            coefs = []
            for h, j in enumerate(sources):
                numer_real = jnp.sum(acc[h][0], axis=1, keepdims=True) / frames
                numer_imag = jnp.sum(acc[h][1], axis=1, keepdims=True) / frames
                denom = jnp.sum(acc[h][2], axis=1, keepdims=True) / frames
                is_self = j == k
                coef_real = jnp.where(is_self, 1.0 - lax.rsqrt(denom), numer_real / denom)
                coef_imag = jnp.where(is_self, 0.0, numer_imag / denom)
                coefs.append((coef_real, coef_imag))
            for c in range(chunks):
                sl = pl.ds(c * chunk, chunk)
                b_r = pr[:, sl]
                b_i = pi[:, sl]
                for j, (coef_real, coef_imag) in zip(sources, coefs):
                    yr[j, :, sl] = yr[j, :, sl] - (coef_real * b_r - coef_imag * b_i)
                    yi[j, :, sl] = yi[j, :, sl] - (coef_real * b_i + coef_imag * b_r)
            for j, (coef_real, coef_imag) in zip(sources, coefs):
                mr_ref[j] = mr_ref[j] - (coef_real * mkr - coef_imag * mki)
                mi_ref[j] = mi_ref[j] - (coef_real * mki + coef_imag * mkr)
            return carry

        lax.fori_loop(0, count // 6, per_pair, 0)
        return carry

    lax.fori_loop(0, count, step, 0)


def sweep(spec_in, var_in, frames):
    _, count, rows, _ = spec_in.shape
    bins, length = rows // 2, frames
    lanes = 128
    vmem = pl.BlockSpec(memory_space=pltpu.VMEM)
    return pl.pallas_call(
        functools.partial(sweep_kernel, frames),
        out_shape=(
            jax.ShapeDtypeStruct((count, bins, lanes), jnp.float32),
            jax.ShapeDtypeStruct((count, bins, lanes), jnp.float32),
        ),
        in_specs=[vmem, vmem],
        out_specs=(vmem, vmem),
        scratch_shapes=[
            pltpu.VMEM((count, bins, length), jnp.float32),
            pltpu.VMEM((count, bins, length), jnp.float32),
            pltpu.VMEM((count, bins, length), jnp.float32),
            pltpu.VMEM((bins, length), jnp.float32),
            pltpu.VMEM((bins, length), jnp.float32),
            pltpu.VMEM((bins, length), jnp.float32),
        ],
        compiler_params=pltpu.CompilerParams(vmem_limit_bytes=60 * 1024 * 1024),
    )(spec_in, var_in)


def gather_kernel(x_ref, o_ref, send_sem, recv_sem, local_sem):
    n = o_ref.shape[0]
    me = lax.axis_index("frame")
    fq = lax.axis_index("freq")
    barrier = pltpu.get_barrier_semaphore()
    for d in range(1, n):
        peer = lax.rem(me + d, n)
        pl.semaphore_signal(barrier, inc=1, device_id=(fq, peer), device_id_type=pl.DeviceIdType.MESH)
    pl.semaphore_wait(barrier, n - 1)
    local = pltpu.make_async_copy(x_ref, o_ref.at[me], local_sem)
    local.start()
    copies = []
    for d in range(1, n):
        peer = lax.rem(me + d, n)
        copy = pltpu.make_async_remote_copy(
            src_ref=x_ref, dst_ref=o_ref.at[me], send_sem=send_sem.at[d], recv_sem=recv_sem.at[d],
            device_id=(fq, peer), device_id_type=pl.DeviceIdType.MESH,
        )
        copy.start()
        copies.append(copy)
    for d in range(1, n):
        source = lax.rem(me + n - d, n)
        copies[d - 1].wait_send()
        incoming = pltpu.make_async_remote_copy(
            src_ref=x_ref, dst_ref=o_ref.at[source], send_sem=send_sem.at[d], recv_sem=recv_sem.at[d],
            device_id=(fq, source), device_id_type=pl.DeviceIdType.MESH,
        )
        incoming.wait_recv()
    local.wait()


def frame_gather(x, n):
    vmem = pl.BlockSpec(memory_space=pltpu.VMEM)
    return pl.pallas_call(
        gather_kernel,
        out_shape=jax.ShapeDtypeStruct((n,) + x.shape, x.dtype),
        in_specs=[vmem],
        out_specs=vmem,
        scratch_shapes=[
            pltpu.SemaphoreType.DMA((n,)),
            pltpu.SemaphoreType.DMA((n,)),
            pltpu.SemaphoreType.DMA,
        ],
        compiler_params=pltpu.CompilerParams(collective_id=0, has_side_effects=True),
    )(x)


def on_device(spectra, norm_gain, w_in, b_in, w_mid, b_mid, w_out, b_out):
    count = spectra.shape[1]
    frames = spectra.shape[3] * lax.axis_size("frame")
    variances = source_model(spectra, norm_gain, w_in, b_in, w_mid, b_mid, w_out, b_out)

    peers = lax.axis_size("frame")
    _, _, freq, span = spectra.shape
    bins = freq // peers
    spec_send = spectra.reshape(2, count, peers, bins, span).transpose(2, 1, 0, 3, 4)
    spec_send = spec_send.reshape(peers, count, 2 * bins, span)
    var_send = variances.reshape(count // 2, 2, peers, bins, span).transpose(2, 0, 1, 3, 4)
    var_send = var_send.reshape(peers, count // 2, 2 * bins, span)
    spec_in = lax.all_to_all(spec_send, "frame", split_axis=0, concat_axis=0, tiled=True)
    var_in = lax.all_to_all(var_send, "frame", split_axis=0, concat_axis=0, tiled=True)
    mix_real, mix_imag = sweep(spec_in, var_in, frames)
    mix = jnp.stack([mix_real[:, :, :count], mix_imag[:, :, :count]])
    peers = lax.axis_size("frame")
    bins = mix.shape[2]
    mix = frame_gather(mix.reshape(-1, 128), peers)
    mix = mix.reshape(peers, 2, count, bins, count).transpose(1, 2, 0, 3, 4)
    mix = mix.reshape(2, count, peers * bins, count)
    mix_real, mix_imag = mix[0], mix[1]
    top = jnp.concatenate([mix_real, -mix_imag], axis=2)
    bottom = jnp.concatenate([mix_imag, mix_real], axis=2)
    mix = jnp.concatenate([top, bottom], axis=0)
    stacked = spectra.reshape(2 * count, spectra.shape[2], spectra.shape[3]).astype(jnp.float32)
    demixed = jnp.einsum(
        "jfa,aft->jft", mix, stacked, precision=lax.Precision.HIGH,
        preferred_element_type=jnp.float32,
    )
    return (demixed.reshape(spectra.shape), variances)


def solution(mesh):
    in_specs = (P(None, None, "freq", "frame"), P(), P(), P(), P(), P(), P(), P())
    out_specs = (P(None, None, "freq", "frame"), P(None, "freq", "frame"))
    return jax.shard_map(
        on_device, mesh=mesh, in_specs=in_specs, out_specs=out_specs, check_vma=False
    )
```

```python
import functools

import jax
import jax.numpy as jnp
from jax import lax
from jax.experimental import pallas as pl
from jax.experimental.pallas import tpu as pltpu
from jax.sharding import PartitionSpec as P

epsilon = 1e-05
power_floor = 0.001
variance_floor = 0.25


def source_model(spectra, norm_gain, w_in, b_in, w_mid, b_mid, w_out, b_out):
    real_part = spectra[0].astype(jnp.float32)
    imag_part = spectra[1].astype(jnp.float32)
    logpower = jnp.log(real_part * real_part + imag_part * imag_part + power_floor).astype(
        jnp.bfloat16
    )
    count, freq, span = logpower.shape
    shards = lax.axis_size("freq")
    rows = span // shards
    send = logpower.transpose(0, 2, 1).reshape(count, shards, rows, freq).transpose(1, 0, 2, 3)
    received = lax.all_to_all(send, "freq", split_axis=0, concat_axis=0, tiled=True)
    values = received.transpose(1, 2, 0, 3).reshape(count, rows, shards * freq).astype(jnp.float32)
    average = jnp.mean(values, axis=2, keepdims=True)
    centred = values - average
    spread = jnp.mean(centred * centred, axis=2, keepdims=True)
    normed = (centred * lax.rsqrt(spread + epsilon) * norm_gain).astype(jnp.bfloat16)
    hidden_one = jax.nn.silu(
        jnp.einsum("ntf,fh->nth", normed, w_in, preferred_element_type=jnp.float32) + b_in
    ).astype(jnp.bfloat16)
    hidden_two = jax.nn.silu(
        jnp.einsum("nth,hg->ntg", hidden_one, w_mid, preferred_element_type=jnp.float32) + b_mid
    ).astype(jnp.bfloat16)
    output_pre = (
        jnp.einsum("nth,hf->ntf", hidden_two, w_out, preferred_element_type=jnp.float32) + b_out
    )
    frame_variances = (jax.nn.softplus(output_pre) + variance_floor).astype(jnp.bfloat16)
    send = frame_variances.reshape(count, rows, shards, freq).transpose(2, 0, 1, 3)
    received = lax.all_to_all(send, "freq", split_axis=0, concat_axis=0, tiled=True)
    return received.transpose(1, 3, 0, 2).reshape(count, freq, span)


def sweep_kernel(frames, spec_in, var_in, mr_ref, mi_ref, yr, yi, w, pr, pi, qr, qi, qp, cr, ci):
    count, bins, length = yr.shape
    peers, _, _, span = spec_in.shape
    chunk = 256
    chunks = length // chunk
    group = 6

    def init(s, carry):
        cols = pl.ds(pl.multiple_of(s * span, span), span)

        def per_pair(p, carry):
            block = var_in[s, p].astype(jnp.float32)
            w[2 * p, :, cols] = 1.0 / block[:bins]
            w[2 * p + 1, :, cols] = 1.0 / block[bins:]
            for half in range(2):
                j = 2 * p + half
                spec = spec_in[s, j].astype(jnp.float32)
                yr[j, :, cols] = spec[:bins]
                yi[j, :, cols] = spec[bins:]
            return carry

        lax.fori_loop(0, count // 2, per_pair, 0)
        return carry

    lax.fori_loop(0, peers, init, 0)

    def init_mix(j, carry):
        lane = lax.broadcasted_iota(jnp.int32, (bins, mr_ref.shape[2]), 1)
        mr_ref[j] = jnp.where(lane == j, 1.0, 0.0).astype(jnp.float32)
        mi_ref[j] = jnp.zeros((bins, mr_ref.shape[2]), jnp.float32)
        return carry

    lax.fori_loop(0, count, init_mix, 0)

    def coefficients(acc, j, source):
        numer_real = jnp.sum(acc[0], axis=1, keepdims=True) / frames
        numer_imag = jnp.sum(acc[1], axis=1, keepdims=True) / frames
        denom = jnp.sum(acc[2], axis=1, keepdims=True) / frames
        is_self = j == source
        coef_real = jnp.where(is_self, 1.0 - lax.rsqrt(denom), numer_real / denom)
        coef_imag = jnp.where(is_self, 0.0, numer_imag / denom)
        cr[j] = jnp.broadcast_to(coef_real, (bins, 128))
        ci[j] = jnp.broadcast_to(coef_imag, (bins, 128))

    def accumulate(acc, ww, a_r, a_i, b_r, b_i, b_p):
        acc[0] = acc[0] + ww * (a_r * b_r + a_i * b_i)
        acc[1] = acc[1] + ww * (a_i * b_r - a_r * b_i)
        acc[2] = acc[2] + ww * b_p

    qr[...] = yr[0]
    qi[...] = yi[0]
    qp[...] = qr[...] * qr[...] + qi[...] * qi[...]

    def first(g, carry):
        sources = tuple(group * g + h for h in range(group))
        acc = [[jnp.zeros((bins, chunk), jnp.float32) for _ in range(3)] for _ in sources]
        for c in range(chunks):
            sl = pl.ds(c * chunk, chunk)
            b_r, b_i, b_p = qr[:, sl], qi[:, sl], qp[:, sl]
            for h, j in enumerate(sources):
                accumulate(acc[h], w[j, :, sl], yr[j, :, sl], yi[j, :, sl], b_r, b_i, b_p)
        for h, j in enumerate(sources):
            coefficients(acc[h], j, 0)
        return carry

    lax.fori_loop(0, count // group, first, 0)

    def step(k, carry):
        pr[...] = qr[...]
        pi[...] = qi[...]
        mkr = mr_ref[k]
        mki = mi_ref[k]

        def mix(j, carry):
            c_r = cr[j][:, :1]
            c_i = ci[j][:, :1]
            mr_ref[j] = mr_ref[j] - (c_r * mkr - c_i * mki)
            mi_ref[j] = mi_ref[j] - (c_r * mki + c_i * mkr)
            return carry

        lax.fori_loop(0, count, mix, 0)
        after = lax.min(k + 1, count - 1)
        c_r = cr[after][:, :1]
        c_i = ci[after][:, :1]
        qr[...] = yr[after] - (c_r * pr[...] - c_i * pi[...])
        qi[...] = yi[after] - (c_r * pi[...] + c_i * pr[...])
        qp[...] = qr[...] * qr[...] + qi[...] * qi[...]

        def fused(g, carry):
            sources = tuple(group * g + h for h in range(group))
            coefs = [(cr[j][:, :1], ci[j][:, :1]) for j in sources]
            acc = [[jnp.zeros((bins, chunk), jnp.float32) for _ in range(3)] for _ in sources]
            for c in range(chunks):
                sl = pl.ds(c * chunk, chunk)
                b_r, b_i = pr[:, sl], pi[:, sl]
                n_r, n_i, n_p = qr[:, sl], qi[:, sl], qp[:, sl]
                for h, j in enumerate(sources):
                    coef_real, coef_imag = coefs[h]
                    a_r = yr[j, :, sl] - (coef_real * b_r - coef_imag * b_i)
                    a_i = yi[j, :, sl] - (coef_real * b_i + coef_imag * b_r)
                    yr[j, :, sl] = a_r
                    yi[j, :, sl] = a_i
                    accumulate(acc[h], w[j, :, sl], a_r, a_i, n_r, n_i, n_p)
            for h, j in enumerate(sources):
                coefficients(acc[h], j, k + 1)
            return carry

        lax.fori_loop(0, count // group, fused, 0)
        return carry

    lax.fori_loop(0, count, step, 0)


def sweep(spec_in, var_in, frames):
    _, count, rows, _ = spec_in.shape
    bins, length = rows // 2, frames
    lanes = 128
    vmem = pl.BlockSpec(memory_space=pltpu.VMEM)
    return pl.pallas_call(
        functools.partial(sweep_kernel, frames),
        out_shape=(
            jax.ShapeDtypeStruct((count, bins, lanes), jnp.float32),
            jax.ShapeDtypeStruct((count, bins, lanes), jnp.float32),
        ),
        in_specs=[vmem, vmem],
        out_specs=(vmem, vmem),
        scratch_shapes=[
            pltpu.VMEM((count, bins, length), jnp.float32),
            pltpu.VMEM((count, bins, length), jnp.float32),
            pltpu.VMEM((count, bins, length), jnp.float32),
            pltpu.VMEM((bins, length), jnp.float32),
            pltpu.VMEM((bins, length), jnp.float32),
            pltpu.VMEM((bins, length), jnp.float32),
            pltpu.VMEM((bins, length), jnp.float32),
            pltpu.VMEM((bins, length), jnp.float32),
            pltpu.VMEM((count, bins, lanes), jnp.float32),
            pltpu.VMEM((count, bins, lanes), jnp.float32),
        ],
        compiler_params=pltpu.CompilerParams(vmem_limit_bytes=60 * 1024 * 1024),
    )(spec_in, var_in)


def gather_kernel(x_ref, o_ref, send_sem, recv_sem, local_sem):
    n = o_ref.shape[0]
    me = lax.axis_index("frame")
    fq = lax.axis_index("freq")
    barrier = pltpu.get_barrier_semaphore()
    for d in range(1, n):
        peer = lax.rem(me + d, n)
        pl.semaphore_signal(barrier, inc=1, device_id=(fq, peer), device_id_type=pl.DeviceIdType.MESH)
    pl.semaphore_wait(barrier, n - 1)
    local = pltpu.make_async_copy(x_ref, o_ref.at[me], local_sem)
    local.start()
    copies = []
    for d in range(1, n):
        peer = lax.rem(me + d, n)
        copy = pltpu.make_async_remote_copy(
            src_ref=x_ref, dst_ref=o_ref.at[me], send_sem=send_sem.at[d], recv_sem=recv_sem.at[d],
            device_id=(fq, peer), device_id_type=pl.DeviceIdType.MESH,
        )
        copy.start()
        copies.append(copy)
    for d in range(1, n):
        source = lax.rem(me + n - d, n)
        copies[d - 1].wait_send()
        incoming = pltpu.make_async_remote_copy(
            src_ref=x_ref, dst_ref=o_ref.at[source], send_sem=send_sem.at[d], recv_sem=recv_sem.at[d],
            device_id=(fq, source), device_id_type=pl.DeviceIdType.MESH,
        )
        incoming.wait_recv()
    local.wait()


def frame_gather(x, n):
    vmem = pl.BlockSpec(memory_space=pltpu.VMEM)
    return pl.pallas_call(
        gather_kernel,
        out_shape=jax.ShapeDtypeStruct((n,) + x.shape, x.dtype),
        in_specs=[vmem],
        out_specs=vmem,
        scratch_shapes=[
            pltpu.SemaphoreType.DMA((n,)),
            pltpu.SemaphoreType.DMA((n,)),
            pltpu.SemaphoreType.DMA,
        ],
        compiler_params=pltpu.CompilerParams(collective_id=0, has_side_effects=True),
    )(x)


def on_device(spectra, norm_gain, w_in, b_in, w_mid, b_mid, w_out, b_out):
    count = spectra.shape[1]
    frames = spectra.shape[3] * lax.axis_size("frame")
    variances = source_model(spectra, norm_gain, w_in, b_in, w_mid, b_mid, w_out, b_out)

    peers = lax.axis_size("frame")
    _, _, freq, span = spectra.shape
    bins = freq // peers
    spec_send = spectra.reshape(2, count, peers, bins, span).transpose(2, 1, 0, 3, 4)
    spec_send = spec_send.reshape(peers, count, 2 * bins, span)
    var_send = variances.reshape(count // 2, 2, peers, bins, span).transpose(2, 0, 1, 3, 4)
    var_send = var_send.reshape(peers, count // 2, 2 * bins, span)
    spec_in = lax.all_to_all(spec_send, "frame", split_axis=0, concat_axis=0, tiled=True)
    var_in = lax.all_to_all(var_send, "frame", split_axis=0, concat_axis=0, tiled=True)
    mix_real, mix_imag = sweep(spec_in, var_in, frames)
    mix = jnp.stack([mix_real[:, :, :count], mix_imag[:, :, :count]])
    peers = lax.axis_size("frame")
    bins = mix.shape[2]
    mix = frame_gather(mix.reshape(-1, 128), peers)
    mix = mix.reshape(peers, 2, count, bins, count).transpose(1, 2, 0, 3, 4)
    mix = mix.reshape(2, count, peers * bins, count)
    mix_real, mix_imag = mix[0], mix[1]
    top = jnp.concatenate([mix_real, -mix_imag], axis=2)
    bottom = jnp.concatenate([mix_imag, mix_real], axis=2)
    mix = jnp.concatenate([top, bottom], axis=0)
    stacked = spectra.reshape(2 * count, spectra.shape[2], spectra.shape[3]).astype(jnp.float32)
    demixed = jnp.einsum(
        "jfa,aft->jft", mix, stacked, precision=lax.Precision.HIGH,
        preferred_element_type=jnp.float32,
    )
    return (demixed.reshape(spectra.shape), variances)


def solution(mesh):
    in_specs = (P(None, None, "freq", "frame"), P(), P(), P(), P(), P(), P(), P())
    out_specs = (P(None, None, "freq", "frame"), P(None, "freq", "frame"))
    return jax.shard_map(
        on_device, mesh=mesh, in_specs=in_specs, out_specs=out_specs, check_vma=False
    )
```

```python
import functools

import jax
import jax.numpy as jnp
from jax import lax
from jax.experimental import pallas as pl
from jax.experimental.pallas import tpu as pltpu
from jax.sharding import PartitionSpec as P

epsilon = 1e-05
power_floor = 0.001
variance_floor = 0.25


def source_model(spectra, norm_gain, w_in, b_in, w_mid, b_mid, w_out, b_out):
    real_part = spectra[0].astype(jnp.float32)
    imag_part = spectra[1].astype(jnp.float32)
    logpower = jnp.log(real_part * real_part + imag_part * imag_part + power_floor).astype(
        jnp.bfloat16
    )
    count, freq, span = logpower.shape
    shards = lax.axis_size("freq")
    rows = span // shards
    send = logpower.transpose(0, 2, 1).reshape(count, shards, rows, freq).transpose(1, 0, 2, 3)
    received = lax.all_to_all(send, "freq", split_axis=0, concat_axis=0, tiled=True)
    values = received.transpose(1, 2, 0, 3).reshape(count, rows, shards * freq).astype(jnp.float32)
    average = jnp.mean(values, axis=2, keepdims=True)
    centred = values - average
    spread = jnp.mean(centred * centred, axis=2, keepdims=True)
    normed = (centred * lax.rsqrt(spread + epsilon) * norm_gain).astype(jnp.bfloat16)
    hidden_one = jax.nn.silu(
        jnp.einsum("ntf,fh->nth", normed, w_in, preferred_element_type=jnp.float32) + b_in
    ).astype(jnp.bfloat16)
    hidden_two = jax.nn.silu(
        jnp.einsum("nth,hg->ntg", hidden_one, w_mid, preferred_element_type=jnp.float32) + b_mid
    ).astype(jnp.bfloat16)
    output_pre = (
        jnp.einsum("nth,hf->ntf", hidden_two, w_out, preferred_element_type=jnp.float32) + b_out
    )
    frame_variances = (jax.nn.softplus(output_pre) + variance_floor).astype(jnp.bfloat16)
    send = frame_variances.reshape(count, rows, shards, freq).transpose(2, 0, 1, 3)
    received = lax.all_to_all(send, "freq", split_axis=0, concat_axis=0, tiled=True)
    return received.transpose(1, 3, 0, 2).reshape(count, freq, span)


def sweep_kernel(frames, spec_in, var_in, mr_ref, mi_ref, yr, yi, w, pr, pi, pp):
    count, bins, length = yr.shape
    peers, _, _, span = spec_in.shape
    chunk = 128
    chunks = length // chunk

    def init(s, carry):
        cols = pl.ds(pl.multiple_of(s * span, span), span)

        def per_pair(p, carry):
            block = var_in[s, p].astype(jnp.float32)
            w[2 * p, :, cols] = 1.0 / block[:bins]
            w[2 * p + 1, :, cols] = 1.0 / block[bins:]
            for half in range(2):
                j = 2 * p + half
                spec = spec_in[s, j].astype(jnp.float32)
                yr[j, :, cols] = spec[:bins]
                yi[j, :, cols] = spec[bins:]
            return carry

        lax.fori_loop(0, count // 2, per_pair, 0)
        return carry

    lax.fori_loop(0, peers, init, 0)

    def init_mix(j, carry):
        lane = lax.broadcasted_iota(jnp.int32, (bins, mr_ref.shape[2]), 1)
        mr_ref[j] = jnp.where(lane == j, 1.0, 0.0).astype(jnp.float32)
        mi_ref[j] = jnp.zeros((bins, mr_ref.shape[2]), jnp.float32)
        return carry

    lax.fori_loop(0, count, init_mix, 0)

    def step(k, carry):
        pr[...] = yr[k]
        pi[...] = yi[k]
        pp[...] = pr[...] * pr[...] + pi[...] * pi[...]
        mkr = mr_ref[k]
        mki = mi_ref[k]

        def per_pair(p, carry):
            sources = tuple(12 * p + h for h in range(12))
            acc = [[jnp.zeros((bins, chunk), jnp.float32) for _ in range(3)] for _ in sources]
            for c in range(chunks):
                sl = pl.ds(c * chunk, chunk)
                b_r = pr[:, sl]
                b_i = pi[:, sl]
                b_p = pp[:, sl]
                for h, j in enumerate(sources):
                    a_r = yr[j, :, sl]
                    a_i = yi[j, :, sl]
                    ww = w[j, :, sl]
                    acc[h][0] = acc[h][0] + ww * (a_r * b_r + a_i * b_i)
                    acc[h][1] = acc[h][1] + ww * (a_i * b_r - a_r * b_i)
                    acc[h][2] = acc[h][2] + ww * b_p
            coefs = []
            for h, j in enumerate(sources):
                numer_real = jnp.sum(acc[h][0], axis=1, keepdims=True) / frames
                numer_imag = jnp.sum(acc[h][1], axis=1, keepdims=True) / frames
                denom = jnp.sum(acc[h][2], axis=1, keepdims=True) / frames
                is_self = j == k
                coef_real = jnp.where(is_self, 1.0 - lax.rsqrt(denom), numer_real / denom)
                coef_imag = jnp.where(is_self, 0.0, numer_imag / denom)
                coefs.append((coef_real, coef_imag))
            for c in range(chunks):
                sl = pl.ds(c * chunk, chunk)
                b_r = pr[:, sl]
                b_i = pi[:, sl]
                for j, (coef_real, coef_imag) in zip(sources, coefs):
                    yr[j, :, sl] = yr[j, :, sl] - (coef_real * b_r - coef_imag * b_i)
                    yi[j, :, sl] = yi[j, :, sl] - (coef_real * b_i + coef_imag * b_r)
            for j, (coef_real, coef_imag) in zip(sources, coefs):
                mr_ref[j] = mr_ref[j] - (coef_real * mkr - coef_imag * mki)
                mi_ref[j] = mi_ref[j] - (coef_real * mki + coef_imag * mkr)
            return carry

        lax.fori_loop(0, count // 12, per_pair, 0)
        return carry

    lax.fori_loop(0, count, step, 0)


def sweep(spec_in, var_in, frames):
    _, count, rows, _ = spec_in.shape
    bins, length = rows // 2, frames
    lanes = 128
    vmem = pl.BlockSpec(memory_space=pltpu.VMEM)
    return pl.pallas_call(
        functools.partial(sweep_kernel, frames),
        out_shape=(
            jax.ShapeDtypeStruct((count, bins, lanes), jnp.float32),
            jax.ShapeDtypeStruct((count, bins, lanes), jnp.float32),
        ),
        in_specs=[vmem, vmem],
        out_specs=(vmem, vmem),
        scratch_shapes=[
            pltpu.VMEM((count, bins, length), jnp.float32),
            pltpu.VMEM((count, bins, length), jnp.float32),
            pltpu.VMEM((count, bins, length), jnp.float32),
            pltpu.VMEM((bins, length), jnp.float32),
            pltpu.VMEM((bins, length), jnp.float32),
            pltpu.VMEM((bins, length), jnp.float32),
        ],
        compiler_params=pltpu.CompilerParams(vmem_limit_bytes=60 * 1024 * 1024),
    )(spec_in, var_in)


def gather_kernel(x_ref, o_ref, send_sem, recv_sem, local_sem):
    n = o_ref.shape[0]
    me = lax.axis_index("frame")
    fq = lax.axis_index("freq")
    barrier = pltpu.get_barrier_semaphore()
    for d in range(1, n):
        peer = lax.rem(me + d, n)
        pl.semaphore_signal(barrier, inc=1, device_id=(fq, peer), device_id_type=pl.DeviceIdType.MESH)
    pl.semaphore_wait(barrier, n - 1)
    local = pltpu.make_async_copy(x_ref, o_ref.at[me], local_sem)
    local.start()
    copies = []
    for d in range(1, n):
        peer = lax.rem(me + d, n)
        copy = pltpu.make_async_remote_copy(
            src_ref=x_ref, dst_ref=o_ref.at[me], send_sem=send_sem.at[d], recv_sem=recv_sem.at[d],
            device_id=(fq, peer), device_id_type=pl.DeviceIdType.MESH,
        )
        copy.start()
        copies.append(copy)
    for d in range(1, n):
        source = lax.rem(me + n - d, n)
        copies[d - 1].wait_send()
        incoming = pltpu.make_async_remote_copy(
            src_ref=x_ref, dst_ref=o_ref.at[source], send_sem=send_sem.at[d], recv_sem=recv_sem.at[d],
            device_id=(fq, source), device_id_type=pl.DeviceIdType.MESH,
        )
        incoming.wait_recv()
    local.wait()


def frame_gather(x, n):
    vmem = pl.BlockSpec(memory_space=pltpu.VMEM)
    return pl.pallas_call(
        gather_kernel,
        out_shape=jax.ShapeDtypeStruct((n,) + x.shape, x.dtype),
        in_specs=[vmem],
        out_specs=vmem,
        scratch_shapes=[
            pltpu.SemaphoreType.DMA((n,)),
            pltpu.SemaphoreType.DMA((n,)),
            pltpu.SemaphoreType.DMA,
        ],
        compiler_params=pltpu.CompilerParams(collective_id=0, has_side_effects=True),
    )(x)


def on_device(spectra, norm_gain, w_in, b_in, w_mid, b_mid, w_out, b_out):
    count = spectra.shape[1]
    frames = spectra.shape[3] * lax.axis_size("frame")
    variances = source_model(spectra, norm_gain, w_in, b_in, w_mid, b_mid, w_out, b_out)

    peers = lax.axis_size("frame")
    _, _, freq, span = spectra.shape
    bins = freq // peers
    spec_send = spectra.reshape(2, count, peers, bins, span).transpose(2, 1, 0, 3, 4)
    spec_send = spec_send.reshape(peers, count, 2 * bins, span)
    var_send = variances.reshape(count // 2, 2, peers, bins, span).transpose(2, 0, 1, 3, 4)
    var_send = var_send.reshape(peers, count // 2, 2 * bins, span)
    spec_in = lax.all_to_all(spec_send, "frame", split_axis=0, concat_axis=0, tiled=True)
    var_in = lax.all_to_all(var_send, "frame", split_axis=0, concat_axis=0, tiled=True)
    mix_real, mix_imag = sweep(spec_in, var_in, frames)
    mix = jnp.stack([mix_real[:, :, :count], mix_imag[:, :, :count]])
    peers = lax.axis_size("frame")
    bins = mix.shape[2]
    mix = frame_gather(mix.reshape(-1, 128), peers)
    mix = mix.reshape(peers, 2, count, bins, count).transpose(1, 2, 0, 3, 4)
    mix = mix.reshape(2, count, peers * bins, count)
    mix_real, mix_imag = mix[0], mix[1]
    top = jnp.concatenate([mix_real, -mix_imag], axis=2)
    bottom = jnp.concatenate([mix_imag, mix_real], axis=2)
    mix = jnp.concatenate([top, bottom], axis=0)
    stacked = spectra.reshape(2 * count, spectra.shape[2], spectra.shape[3]).astype(jnp.float32)
    demixed = jnp.einsum(
        "jfa,aft->jft", mix, stacked, precision=lax.Precision.HIGH,
        preferred_element_type=jnp.float32,
    )
    return (demixed.reshape(spectra.shape), variances)


def solution(mesh):
    in_specs = (P(None, None, "freq", "frame"), P(), P(), P(), P(), P(), P(), P())
    out_specs = (P(None, None, "freq", "frame"), P(None, "freq", "frame"))
    return jax.shard_map(
        on_device, mesh=mesh, in_specs=in_specs, out_specs=out_specs, check_vma=False
    )
```

```python
import functools

import jax
import jax.numpy as jnp
from jax import lax
from jax.experimental import pallas as pl
from jax.experimental.pallas import tpu as pltpu
from jax.sharding import PartitionSpec as P

epsilon = 1e-05
power_floor = 0.001
variance_floor = 0.25


def source_model(spectra, norm_gain, w_in, b_in, w_mid, b_mid, w_out, b_out):
    real_part = spectra[0].astype(jnp.float32)
    imag_part = spectra[1].astype(jnp.float32)
    logpower = jnp.log(real_part * real_part + imag_part * imag_part + power_floor).astype(
        jnp.bfloat16
    )
    count, freq, span = logpower.shape
    shards = lax.axis_size("freq")
    rows = span // shards
    send = logpower.transpose(0, 2, 1).reshape(count, shards, rows, freq).transpose(1, 0, 2, 3)
    received = lax.all_to_all(send, "freq", split_axis=0, concat_axis=0, tiled=True)
    values = received.transpose(1, 2, 0, 3).reshape(count, rows, shards * freq).astype(jnp.float32)
    average = jnp.mean(values, axis=2, keepdims=True)
    centred = values - average
    spread = jnp.mean(centred * centred, axis=2, keepdims=True)
    normed = (centred * lax.rsqrt(spread + epsilon) * norm_gain).astype(jnp.bfloat16)
    hidden_one = jax.nn.silu(
        jnp.einsum("ntf,fh->nth", normed, w_in, preferred_element_type=jnp.float32) + b_in
    ).astype(jnp.bfloat16)
    hidden_two = jax.nn.silu(
        jnp.einsum("nth,hg->ntg", hidden_one, w_mid, preferred_element_type=jnp.float32) + b_mid
    ).astype(jnp.bfloat16)
    output_pre = (
        jnp.einsum("nth,hf->ntf", hidden_two, w_out, preferred_element_type=jnp.float32) + b_out
    )
    frame_variances = (jax.nn.softplus(output_pre) + variance_floor).astype(jnp.bfloat16)
    send = frame_variances.reshape(count, rows, shards, freq).transpose(2, 0, 1, 3)
    received = lax.all_to_all(send, "freq", split_axis=0, concat_axis=0, tiled=True)
    return received.transpose(1, 3, 0, 2).reshape(count, freq, span)


def sweep_kernel(frames, spec_in, var_in, mr_ref, mi_ref, yr, yi, w, pr, pi, pp):
    count, bins, length = yr.shape
    peers, _, _, span = spec_in.shape
    chunk = 256
    chunks = length // chunk

    def init(s, carry):
        cols = pl.ds(pl.multiple_of(s * span, span), span)

        def per_pair(p, carry):
            block = var_in[s, p].astype(jnp.float32)
            w[2 * p, :, cols] = 1.0 / block[:bins]
            w[2 * p + 1, :, cols] = 1.0 / block[bins:]
            for half in range(2):
                j = 2 * p + half
                spec = spec_in[s, j].astype(jnp.float32)
                yr[j, :, cols] = spec[:bins]
                yi[j, :, cols] = spec[bins:]
            return carry

        lax.fori_loop(0, count // 2, per_pair, 0)
        return carry

    lax.fori_loop(0, peers, init, 0)

    def init_mix(j, carry):
        lane = lax.broadcasted_iota(jnp.int32, (bins, mr_ref.shape[2]), 1)
        mr_ref[j] = jnp.where(lane == j, 1.0, 0.0).astype(jnp.float32)
        mi_ref[j] = jnp.zeros((bins, mr_ref.shape[2]), jnp.float32)
        return carry

    lax.fori_loop(0, count, init_mix, 0)

    def step(k, carry):
        pr[...] = yr[k]
        pi[...] = yi[k]
        pp[...] = pr[...] * pr[...] + pi[...] * pi[...]
        mkr = mr_ref[k]
        mki = mi_ref[k]

        def per_pair(p, carry):
            sources = tuple(6 * p + h for h in range(6))
            acc = [[jnp.zeros((bins, chunk), jnp.float32) for _ in range(3)] for _ in sources]
            for c in range(chunks):
                sl = pl.ds(c * chunk, chunk)
                b_r = pr[:, sl]
                b_i = pi[:, sl]
                b_p = pp[:, sl]
                for h, j in enumerate(sources):
                    a_r = yr[j, :, sl]
                    a_i = yi[j, :, sl]
                    ww = w[j, :, sl]
                    acc[h][0] = acc[h][0] + ww * (a_r * b_r + a_i * b_i)
                    acc[h][1] = acc[h][1] + ww * (a_i * b_r - a_r * b_i)
                    acc[h][2] = acc[h][2] + ww * b_p
            coefs = []
            for h, j in enumerate(sources):
                numer_real = jnp.sum(acc[h][0], axis=1, keepdims=True) / frames
                numer_imag = jnp.sum(acc[h][1], axis=1, keepdims=True) / frames
                denom = jnp.sum(acc[h][2], axis=1, keepdims=True) / frames
                is_self = j == k
                coef_real = jnp.where(is_self, 1.0 - lax.rsqrt(denom), numer_real / denom)
                coef_imag = jnp.where(is_self, 0.0, numer_imag / denom)
                coefs.append((coef_real, coef_imag))
            for c in range(chunks):
                sl = pl.ds(c * chunk, chunk)
                b_r = pr[:, sl]
                b_i = pi[:, sl]
                for j, (coef_real, coef_imag) in zip(sources, coefs):
                    yr[j, :, sl] = yr[j, :, sl] - (coef_real * b_r - coef_imag * b_i)
                    yi[j, :, sl] = yi[j, :, sl] - (coef_real * b_i + coef_imag * b_r)
            for j, (coef_real, coef_imag) in zip(sources, coefs):
                mr_ref[j] = mr_ref[j] - (coef_real * mkr - coef_imag * mki)
                mi_ref[j] = mi_ref[j] - (coef_real * mki + coef_imag * mkr)
            return carry

        lax.fori_loop(0, count // 6, per_pair, 0)
        return carry

    lax.fori_loop(0, count, step, 0)


def sweep(spec_in, var_in, frames):
    _, count, rows, _ = spec_in.shape
    bins, length = rows // 2, frames
    lanes = 128
    vmem = pl.BlockSpec(memory_space=pltpu.VMEM)
    return pl.pallas_call(
        functools.partial(sweep_kernel, frames),
        out_shape=(
            jax.ShapeDtypeStruct((count, bins, lanes), jnp.float32),
            jax.ShapeDtypeStruct((count, bins, lanes), jnp.float32),
        ),
        in_specs=[vmem, vmem],
        out_specs=(vmem, vmem),
        scratch_shapes=[
            pltpu.VMEM((count, bins, length), jnp.float32),
            pltpu.VMEM((count, bins, length), jnp.float32),
            pltpu.VMEM((count, bins, length), jnp.float32),
            pltpu.VMEM((bins, length), jnp.float32),
            pltpu.VMEM((bins, length), jnp.float32),
            pltpu.VMEM((bins, length), jnp.float32),
        ],
        compiler_params=pltpu.CompilerParams(vmem_limit_bytes=60 * 1024 * 1024),
    )(spec_in, var_in)


def gather_kernel(x_ref, o_ref, send_sem, recv_sem, local_sem):
    n = o_ref.shape[0]
    me = lax.axis_index("frame")
    fq = lax.axis_index("freq")
    barrier = pltpu.get_barrier_semaphore()
    for d in range(1, n):
        peer = lax.rem(me + d, n)
        pl.semaphore_signal(barrier, inc=1, device_id=(fq, peer), device_id_type=pl.DeviceIdType.MESH)
    pl.semaphore_wait(barrier, n - 1)
    local = pltpu.make_async_copy(x_ref, o_ref.at[me], local_sem)
    local.start()
    copies = []
    for d in range(1, n):
        peer = lax.rem(me + d, n)
        copy = pltpu.make_async_remote_copy(
            src_ref=x_ref, dst_ref=o_ref.at[me], send_sem=send_sem.at[d], recv_sem=recv_sem.at[d],
            device_id=(fq, peer), device_id_type=pl.DeviceIdType.MESH,
        )
        copy.start()
        copies.append(copy)
    for d in range(1, n):
        source = lax.rem(me + n - d, n)
        copies[d - 1].wait_send()
        incoming = pltpu.make_async_remote_copy(
            src_ref=x_ref, dst_ref=o_ref.at[source], send_sem=send_sem.at[d], recv_sem=recv_sem.at[d],
            device_id=(fq, source), device_id_type=pl.DeviceIdType.MESH,
        )
        incoming.wait_recv()
    local.wait()


def frame_gather(x, n):
    vmem = pl.BlockSpec(memory_space=pltpu.VMEM)
    return pl.pallas_call(
        gather_kernel,
        out_shape=jax.ShapeDtypeStruct((n,) + x.shape, x.dtype),
        in_specs=[vmem],
        out_specs=vmem,
        scratch_shapes=[
            pltpu.SemaphoreType.DMA((n,)),
            pltpu.SemaphoreType.DMA((n,)),
            pltpu.SemaphoreType.DMA,
        ],
        compiler_params=pltpu.CompilerParams(collective_id=0, has_side_effects=True),
    )(x)


def on_device(spectra, norm_gain, w_in, b_in, w_mid, b_mid, w_out, b_out):
    count = spectra.shape[1]
    frames = spectra.shape[3] * lax.axis_size("frame")
    variances = source_model(spectra, norm_gain, w_in, b_in, w_mid, b_mid, w_out, b_out)

    peers = lax.axis_size("frame")
    _, _, freq, span = spectra.shape
    bins = freq // peers
    spec_send = spectra.reshape(2, count, peers, bins, span).transpose(2, 1, 0, 3, 4)
    spec_send = spec_send.reshape(peers, count, 2 * bins, span)
    var_send = variances.reshape(count // 2, 2, peers, bins, span).transpose(2, 0, 1, 3, 4)
    var_send = var_send.reshape(peers, count // 2, 2 * bins, span)
    spec_in = lax.all_to_all(spec_send, "frame", split_axis=0, concat_axis=0, tiled=True)
    var_in = lax.all_to_all(var_send, "frame", split_axis=0, concat_axis=0, tiled=True)
    mix_real, mix_imag = sweep(spec_in, var_in, frames)
    mix = jnp.stack([mix_real[:, :, :count], mix_imag[:, :, :count]])
    peers = lax.axis_size("frame")
    bins = mix.shape[2]
    mix = frame_gather(mix.reshape(-1, 128), peers)
    mix = mix.reshape(peers, 2, count, bins, count).transpose(1, 2, 0, 3, 4)
    mix = mix.reshape(2, count, peers * bins, count)
    mix_real, mix_imag = mix[0], mix[1]
    top = jnp.concatenate([mix_real, -mix_imag], axis=2)
    bottom = jnp.concatenate([mix_imag, mix_real], axis=2)
    mix = jnp.concatenate([top, bottom], axis=0)
    stacked = spectra.reshape(2 * count, spectra.shape[2], spectra.shape[3])
    mix_high = mix.astype(jnp.bfloat16)
    mix_low = (mix - mix_high.astype(jnp.float32)).astype(jnp.bfloat16)
    demixed = jnp.einsum(
        "jfa,aft->jft", mix_high, stacked, preferred_element_type=jnp.float32
    ) + jnp.einsum("jfa,aft->jft", mix_low, stacked, preferred_element_type=jnp.float32)
    return (demixed.reshape(spectra.shape), variances)


def solution(mesh):
    in_specs = (P(None, None, "freq", "frame"), P(), P(), P(), P(), P(), P(), P())
    out_specs = (P(None, None, "freq", "frame"), P(None, "freq", "frame"))
    return jax.shard_map(
        on_device, mesh=mesh, in_specs=in_specs, out_specs=out_specs, check_vma=False
    )
```

```python
import functools

import jax
import jax.numpy as jnp
from jax import lax
from jax.experimental import pallas as pl
from jax.experimental.pallas import tpu as pltpu
from jax.sharding import PartitionSpec as P

epsilon = 1e-05
power_floor = 0.001
variance_floor = 0.25


def source_model(spectra, norm_gain, w_in, b_in, w_mid, b_mid, w_out, b_out):
    real_part = spectra[0].astype(jnp.float32)
    imag_part = spectra[1].astype(jnp.float32)
    logpower = jnp.log(real_part * real_part + imag_part * imag_part + power_floor).astype(
        jnp.bfloat16
    )
    count, freq, span = logpower.shape
    shards = lax.axis_size("freq")
    rows = span // shards
    send = logpower.transpose(0, 2, 1).reshape(count, shards, rows, freq).transpose(1, 0, 2, 3)
    received = lax.all_to_all(send, "freq", split_axis=0, concat_axis=0, tiled=True)
    values = received.transpose(1, 2, 0, 3).reshape(count, rows, shards * freq).astype(jnp.float32)
    average = jnp.mean(values, axis=2, keepdims=True)
    centred = values - average
    spread = jnp.mean(centred * centred, axis=2, keepdims=True)
    normed = (centred * lax.rsqrt(spread + epsilon) * norm_gain).astype(jnp.bfloat16)
    hidden_one = jax.nn.silu(
        jnp.einsum("ntf,fh->nth", normed, w_in, preferred_element_type=jnp.float32) + b_in
    ).astype(jnp.bfloat16)
    hidden_two = jax.nn.silu(
        jnp.einsum("nth,hg->ntg", hidden_one, w_mid, preferred_element_type=jnp.float32) + b_mid
    ).astype(jnp.bfloat16)
    output_pre = (
        jnp.einsum("nth,hf->ntf", hidden_two, w_out, preferred_element_type=jnp.float32) + b_out
    )
    frame_variances = (jax.nn.softplus(output_pre) + variance_floor).astype(jnp.bfloat16)
    send = frame_variances.reshape(count, rows, shards, freq).transpose(2, 0, 1, 3)
    received = lax.all_to_all(send, "freq", split_axis=0, concat_axis=0, tiled=True)
    return received.transpose(1, 3, 0, 2).reshape(count, freq, span)


def sweep_kernel(frames, spec_in, var_in, mr_ref, mi_ref, yr, yi, w, pr, pi, pp):
    count, bins, length = yr.shape
    peers, _, _, span = spec_in.shape
    chunk = 256
    chunks = length // chunk

    def init(s, carry):
        cols = pl.ds(pl.multiple_of(s * span, span), span)

        def per_pair(p, carry):
            block = var_in[s, p].astype(jnp.float32)
            w[2 * p, :, cols] = 1.0 / block[:bins]
            w[2 * p + 1, :, cols] = 1.0 / block[bins:]
            for half in range(2):
                j = 2 * p + half
                spec = spec_in[s, j].astype(jnp.float32)
                yr[j, :, cols] = spec[:bins]
                yi[j, :, cols] = spec[bins:]
            return carry

        lax.fori_loop(0, count // 2, per_pair, 0)
        return carry

    lax.fori_loop(0, peers, init, 0)

    def init_mix(j, carry):
        lane = lax.broadcasted_iota(jnp.int32, (bins, mr_ref.shape[2]), 1)
        mr_ref[j] = jnp.where(lane == j, 1.0, 0.0).astype(jnp.float32)
        mi_ref[j] = jnp.zeros((bins, mr_ref.shape[2]), jnp.float32)
        return carry

    lax.fori_loop(0, count, init_mix, 0)

    def step(k, carry):
        pr[...] = yr[k]
        pi[...] = yi[k]
        pp[...] = pr[...] * pr[...] + pi[...] * pi[...]
        mkr = mr_ref[k]
        mki = mi_ref[k]

        def per_pair(p, carry):
            sources = tuple(6 * p + h for h in range(6))
            acc = [[jnp.zeros((bins, chunk), jnp.float32) for _ in range(3)] for _ in sources]
            for c in range(chunks):
                sl = pl.ds(c * chunk, chunk)
                b_r = pr[:, sl]
                b_i = pi[:, sl]
                b_p = pp[:, sl]
                for h, j in enumerate(sources):
                    a_r = yr[j, :, sl]
                    a_i = yi[j, :, sl]
                    ww = w[j, :, sl]
                    acc[h][0] = acc[h][0] + ww * (a_r * b_r + a_i * b_i)
                    acc[h][1] = acc[h][1] + ww * (a_i * b_r - a_r * b_i)
                    acc[h][2] = acc[h][2] + ww * b_p
            coefs = []
            for h, j in enumerate(sources):
                numer_real = jnp.sum(acc[h][0], axis=1, keepdims=True) / frames
                numer_imag = jnp.sum(acc[h][1], axis=1, keepdims=True) / frames
                denom = jnp.sum(acc[h][2], axis=1, keepdims=True) / frames
                is_self = j == k
                coef_real = jnp.where(is_self, 1.0 - lax.rsqrt(denom), numer_real / denom)
                coef_imag = jnp.where(is_self, 0.0, numer_imag / denom)
                coefs.append((coef_real, coef_imag))
            for c in range(chunks):
                sl = pl.ds(c * chunk, chunk)
                b_r = pr[:, sl]
                b_i = pi[:, sl]
                for j, (coef_real, coef_imag) in zip(sources, coefs):
                    yr[j, :, sl] = yr[j, :, sl] - (coef_real * b_r - coef_imag * b_i)
                    yi[j, :, sl] = yi[j, :, sl] - (coef_real * b_i + coef_imag * b_r)
            for j, (coef_real, coef_imag) in zip(sources, coefs):
                mr_ref[j] = mr_ref[j] - (coef_real * mkr - coef_imag * mki)
                mi_ref[j] = mi_ref[j] - (coef_real * mki + coef_imag * mkr)
            return carry

        lax.fori_loop(0, count // 6, per_pair, 0)
        return carry

    lax.fori_loop(0, count, step, 0)


def sweep(spec_in, var_in, frames):
    _, count, rows, _ = spec_in.shape
    bins, length = rows // 2, frames
    lanes = 128
    vmem = pl.BlockSpec(memory_space=pltpu.VMEM)
    return pl.pallas_call(
        functools.partial(sweep_kernel, frames),
        out_shape=(
            jax.ShapeDtypeStruct((count, bins, lanes), jnp.float32),
            jax.ShapeDtypeStruct((count, bins, lanes), jnp.float32),
        ),
        in_specs=[vmem, vmem],
        out_specs=(vmem, vmem),
        scratch_shapes=[
            pltpu.VMEM((count, bins, length), jnp.float32),
            pltpu.VMEM((count, bins, length), jnp.float32),
            pltpu.VMEM((count, bins, length), jnp.float32),
            pltpu.VMEM((bins, length), jnp.float32),
            pltpu.VMEM((bins, length), jnp.float32),
            pltpu.VMEM((bins, length), jnp.float32),
        ],
        compiler_params=pltpu.CompilerParams(vmem_limit_bytes=60 * 1024 * 1024),
    )(spec_in, var_in)


def gather_kernel(x_ref, o_ref, send_sem, recv_sem, local_sem):
    n = o_ref.shape[0]
    me = lax.axis_index("frame")
    fq = lax.axis_index("freq")
    barrier = pltpu.get_barrier_semaphore()
    for d in range(1, n):
        peer = lax.rem(me + d, n)
        pl.semaphore_signal(barrier, inc=1, device_id=(fq, peer), device_id_type=pl.DeviceIdType.MESH)
    pl.semaphore_wait(barrier, n - 1)
    local = pltpu.make_async_copy(x_ref, o_ref.at[me], local_sem)
    local.start()
    copies = []
    for d in range(1, n):
        peer = lax.rem(me + d, n)
        copy = pltpu.make_async_remote_copy(
            src_ref=x_ref, dst_ref=o_ref.at[me], send_sem=send_sem.at[d], recv_sem=recv_sem.at[d],
            device_id=(fq, peer), device_id_type=pl.DeviceIdType.MESH,
        )
        copy.start()
        copies.append(copy)
    for d in range(1, n):
        source = lax.rem(me + n - d, n)
        copies[d - 1].wait_send()
        incoming = pltpu.make_async_remote_copy(
            src_ref=x_ref, dst_ref=o_ref.at[source], send_sem=send_sem.at[d], recv_sem=recv_sem.at[d],
            device_id=(fq, source), device_id_type=pl.DeviceIdType.MESH,
        )
        incoming.wait_recv()
    local.wait()


def frame_gather(x, n):
    vmem = pl.BlockSpec(memory_space=pltpu.VMEM)
    return pl.pallas_call(
        gather_kernel,
        out_shape=jax.ShapeDtypeStruct((n,) + x.shape, x.dtype),
        in_specs=[vmem],
        out_specs=vmem,
        scratch_shapes=[
            pltpu.SemaphoreType.DMA((n,)),
            pltpu.SemaphoreType.DMA((n,)),
            pltpu.SemaphoreType.DMA,
        ],
        compiler_params=pltpu.CompilerParams(collective_id=0, has_side_effects=True),
    )(x)


def on_device(spectra, norm_gain, w_in, b_in, w_mid, b_mid, w_out, b_out):
    count = spectra.shape[1]
    frames = spectra.shape[3] * lax.axis_size("frame")
    variances = source_model(spectra, norm_gain, w_in, b_in, w_mid, b_mid, w_out, b_out)

    peers = lax.axis_size("frame")
    _, _, freq, span = spectra.shape
    bins = freq // peers
    spec_send = spectra.reshape(2, count, peers, bins, span).transpose(2, 1, 0, 3, 4)
    spec_send = spec_send.reshape(peers, count, 2 * bins, span)
    var_send = variances.reshape(count // 2, 2, peers, bins, span).transpose(2, 0, 1, 3, 4)
    var_send = var_send.reshape(peers, count // 2, 2 * bins, span)
    spec_in = lax.all_to_all(spec_send, "frame", split_axis=0, concat_axis=0, tiled=True)
    var_in = lax.all_to_all(var_send, "frame", split_axis=0, concat_axis=0, tiled=True)
    mix_real, mix_imag = sweep(spec_in, var_in, frames)
    mix = jnp.stack([mix_real[:, :, :count], mix_imag[:, :, :count]])
    peers = lax.axis_size("frame")
    bins = mix.shape[2]
    mix = frame_gather(mix.reshape(-1, 128), peers)
    mix = mix.reshape(peers, 2, count, bins, count).transpose(1, 2, 0, 3, 4)
    mix = mix.reshape(2, count, peers * bins, count)
    mix_real, mix_imag = mix[0], mix[1]
    real_part = spectra[0].astype(jnp.float32)
    imag_part = spectra[1].astype(jnp.float32)

    def apply(m, y):
        return jnp.einsum(
            "jfa,aft->jft", m, y, precision=lax.Precision.HIGH, preferred_element_type=jnp.float32
        )

    demixed_real = apply(mix_real, real_part) - apply(mix_imag, imag_part)
    demixed_imag = apply(mix_real, imag_part) + apply(mix_imag, real_part)
    return (jnp.stack([demixed_real, demixed_imag]), variances)


def solution(mesh):
    in_specs = (P(None, None, "freq", "frame"), P(), P(), P(), P(), P(), P(), P())
    out_specs = (P(None, None, "freq", "frame"), P(None, "freq", "frame"))
    return jax.shard_map(
        on_device, mesh=mesh, in_specs=in_specs, out_specs=out_specs, check_vma=False
    )
```

```python
import functools

import jax
import jax.numpy as jnp
from jax import lax
from jax.experimental import pallas as pl
from jax.experimental.pallas import tpu as pltpu
from jax.sharding import PartitionSpec as P

epsilon = 1e-05
power_floor = 0.001
variance_floor = 0.25


def source_model(spectra, norm_gain, w_in, b_in, w_mid, b_mid, w_out, b_out):
    real_part = spectra[0].astype(jnp.float32)
    imag_part = spectra[1].astype(jnp.float32)
    logpower = jnp.log(real_part * real_part + imag_part * imag_part + power_floor).astype(
        jnp.bfloat16
    )
    count, freq, span = logpower.shape
    shards = lax.axis_size("freq")
    rows = span // shards
    send = logpower.transpose(0, 2, 1).reshape(count, shards, rows, freq).transpose(1, 0, 2, 3)
    received = lax.all_to_all(send, "freq", split_axis=0, concat_axis=0, tiled=True)
    values = received.transpose(1, 2, 0, 3).reshape(count, rows, shards * freq).astype(jnp.float32)
    average = jnp.mean(values, axis=2, keepdims=True)
    centred = values - average
    spread = jnp.mean(centred * centred, axis=2, keepdims=True)
    normed = (centred * lax.rsqrt(spread + epsilon) * norm_gain).astype(jnp.bfloat16)
    hidden_one = jax.nn.silu(
        jnp.einsum("ntf,fh->nth", normed, w_in, preferred_element_type=jnp.float32) + b_in
    ).astype(jnp.bfloat16)
    hidden_two = jax.nn.silu(
        jnp.einsum("nth,hg->ntg", hidden_one, w_mid, preferred_element_type=jnp.float32) + b_mid
    ).astype(jnp.bfloat16)
    output_pre = (
        jnp.einsum("nth,hf->ntf", hidden_two, w_out, preferred_element_type=jnp.float32) + b_out
    )
    frame_variances = (jax.nn.softplus(output_pre) + variance_floor).astype(jnp.bfloat16)
    send = frame_variances.reshape(count, rows, shards, freq).transpose(2, 0, 1, 3)
    received = lax.all_to_all(send, "freq", split_axis=0, concat_axis=0, tiled=True)
    return received.transpose(1, 3, 0, 2).reshape(count, freq, span)


def sweep_kernel(frames, spec_in, var_in, mr_ref, mi_ref, yr, yi, w, pr, pi, pp):
    count, bins, length = yr.shape
    peers, _, _, span = spec_in.shape
    chunk = 256
    chunks = length // chunk

    def init(s, carry):
        cols = pl.ds(pl.multiple_of(s * span, span), span)

        def per_pair(p, carry):
            block = var_in[s, p].astype(jnp.float32)
            w[2 * p, :, cols] = 1.0 / block[:bins]
            w[2 * p + 1, :, cols] = 1.0 / block[bins:]
            for half in range(2):
                j = 2 * p + half
                spec = spec_in[s, j].astype(jnp.float32)
                yr[j, :, cols] = spec[:bins]
                yi[j, :, cols] = spec[bins:]
            return carry

        lax.fori_loop(0, count // 2, per_pair, 0)
        return carry

    lax.fori_loop(0, peers, init, 0)

    def init_mix(j, carry):
        lane = lax.broadcasted_iota(jnp.int32, (bins, mr_ref.shape[2]), 1)
        mr_ref[j] = jnp.where(lane == j, 1.0, 0.0).astype(jnp.float32)
        mi_ref[j] = jnp.zeros((bins, mr_ref.shape[2]), jnp.float32)
        return carry

    lax.fori_loop(0, count, init_mix, 0)

    def step(k, carry):
        pr[...] = yr[k]
        pi[...] = yi[k]
        pp[...] = pr[...] * pr[...] + pi[...] * pi[...]
        mkr = mr_ref[k]
        mki = mi_ref[k]

        def per_pair(p, carry):
            sources = tuple(6 * p + h for h in range(6))
            acc = [[jnp.zeros((bins, chunk), jnp.float32) for _ in range(3)] for _ in sources]
            for c in range(chunks):
                sl = pl.ds(c * chunk, chunk)
                b_r = pr[:, sl]
                b_i = pi[:, sl]
                b_p = pp[:, sl]
                for h, j in enumerate(sources):
                    a_r = yr[j, :, sl]
                    a_i = yi[j, :, sl]
                    ww = w[j, :, sl]
                    acc[h][0] = acc[h][0] + ww * (a_r * b_r + a_i * b_i)
                    acc[h][1] = acc[h][1] + ww * (a_i * b_r - a_r * b_i)
                    acc[h][2] = acc[h][2] + ww * b_p
            coefs = []
            for h, j in enumerate(sources):
                numer_real = jnp.sum(acc[h][0], axis=1, keepdims=True) / frames
                numer_imag = jnp.sum(acc[h][1], axis=1, keepdims=True) / frames
                denom = jnp.sum(acc[h][2], axis=1, keepdims=True) / frames
                is_self = j == k
                coef_real = jnp.where(is_self, 1.0 - lax.rsqrt(denom), numer_real / denom)
                coef_imag = jnp.where(is_self, 0.0, numer_imag / denom)
                coefs.append((coef_real, coef_imag))
            for c in range(chunks):
                sl = pl.ds(c * chunk, chunk)
                b_r = pr[:, sl]
                b_i = pi[:, sl]
                for j, (coef_real, coef_imag) in zip(sources, coefs):
                    yr[j, :, sl] = yr[j, :, sl] - (coef_real * b_r - coef_imag * b_i)
                    yi[j, :, sl] = yi[j, :, sl] - (coef_real * b_i + coef_imag * b_r)
            for j, (coef_real, coef_imag) in zip(sources, coefs):
                mr_ref[j] = mr_ref[j] - (coef_real * mkr - coef_imag * mki)
                mi_ref[j] = mi_ref[j] - (coef_real * mki + coef_imag * mkr)
            return carry

        lax.fori_loop(0, count // 6, per_pair, 0)
        return carry

    lax.fori_loop(0, count, step, 0)


def sweep(spec_in, var_in, frames):
    _, count, rows, _ = spec_in.shape
    bins, length = rows // 2, frames
    lanes = 128
    vmem = pl.BlockSpec(memory_space=pltpu.VMEM)
    return pl.pallas_call(
        functools.partial(sweep_kernel, frames),
        out_shape=(
            jax.ShapeDtypeStruct((count, bins, lanes), jnp.float32),
            jax.ShapeDtypeStruct((count, bins, lanes), jnp.float32),
        ),
        in_specs=[vmem, vmem],
        out_specs=(vmem, vmem),
        scratch_shapes=[
            pltpu.VMEM((count, bins, length), jnp.float32),
            pltpu.VMEM((count, bins, length), jnp.float32),
            pltpu.VMEM((count, bins, length), jnp.float32),
            pltpu.VMEM((bins, length), jnp.float32),
            pltpu.VMEM((bins, length), jnp.float32),
            pltpu.VMEM((bins, length), jnp.float32),
        ],
        compiler_params=pltpu.CompilerParams(vmem_limit_bytes=60 * 1024 * 1024),
    )(spec_in, var_in)


def gather_kernel(x_ref, o_ref, send_sem, recv_sem, local_sem):
    n = o_ref.shape[0]
    me = lax.axis_index("frame")
    fq = lax.axis_index("freq")
    barrier = pltpu.get_barrier_semaphore()
    for d in range(1, n):
        peer = lax.rem(me + d, n)
        pl.semaphore_signal(barrier, inc=1, device_id=(fq, peer), device_id_type=pl.DeviceIdType.MESH)
    pl.semaphore_wait(barrier, n - 1)
    local = pltpu.make_async_copy(x_ref, o_ref.at[me], local_sem)
    local.start()
    copies = []
    for d in range(1, n):
        peer = lax.rem(me + d, n)
        copy = pltpu.make_async_remote_copy(
            src_ref=x_ref, dst_ref=o_ref.at[me], send_sem=send_sem.at[d], recv_sem=recv_sem.at[d],
            device_id=(fq, peer), device_id_type=pl.DeviceIdType.MESH,
        )
        copy.start()
        copies.append(copy)
    for d in range(1, n):
        source = lax.rem(me + n - d, n)
        copies[d - 1].wait_send()
        incoming = pltpu.make_async_remote_copy(
            src_ref=x_ref, dst_ref=o_ref.at[source], send_sem=send_sem.at[d], recv_sem=recv_sem.at[d],
            device_id=(fq, source), device_id_type=pl.DeviceIdType.MESH,
        )
        incoming.wait_recv()
    local.wait()


def frame_gather(x, n):
    vmem = pl.BlockSpec(memory_space=pltpu.VMEM)
    return pl.pallas_call(
        gather_kernel,
        out_shape=jax.ShapeDtypeStruct((n,) + x.shape, x.dtype),
        in_specs=[vmem],
        out_specs=vmem,
        scratch_shapes=[
            pltpu.SemaphoreType.DMA((n,)),
            pltpu.SemaphoreType.DMA((n,)),
            pltpu.SemaphoreType.DMA,
        ],
        compiler_params=pltpu.CompilerParams(collective_id=0, has_side_effects=True),
    )(x)


def on_device(spectra, norm_gain, w_in, b_in, w_mid, b_mid, w_out, b_out):
    count = spectra.shape[1]
    frames = spectra.shape[3] * lax.axis_size("frame")
    variances = source_model(spectra, norm_gain, w_in, b_in, w_mid, b_mid, w_out, b_out)

    peers = lax.axis_size("frame")
    _, _, freq, span = spectra.shape
    bins = freq // peers
    spec_send = spectra.reshape(2, count, peers, bins, span).transpose(2, 1, 0, 3, 4)
    spec_send = spec_send.reshape(peers, count, 2 * bins, span)
    var_send = variances.reshape(count // 2, 2, peers, bins, span).transpose(2, 0, 1, 3, 4)
    var_send = var_send.reshape(peers, count // 2, 2 * bins, span)
    spec_in = lax.all_to_all(spec_send, "frame", split_axis=0, concat_axis=0, tiled=True)
    var_in = lax.all_to_all(var_send, "frame", split_axis=0, concat_axis=0, tiled=True)
    mix_real, mix_imag = sweep(spec_in, var_in, frames)
    mix = jnp.stack([mix_real[:, :, :count], mix_imag[:, :, :count]])
    peers = lax.axis_size("frame")
    bins = mix.shape[2]
    mix = frame_gather(mix.reshape(-1, 128), peers)
    mix = mix.reshape(peers, 2, count, bins, count)
    mix_real, mix_imag = mix[:, 0], mix[:, 1]
    view = (count, peers, bins, spectra.shape[3])
    real_part = spectra[0].astype(jnp.float32).reshape(view)
    imag_part = spectra[1].astype(jnp.float32).reshape(view)

    def apply(m, y):
        out = jnp.einsum(
            "sjba,asbt->jsbt", m, y, precision=lax.Precision.HIGH,
            preferred_element_type=jnp.float32,
        )
        return out.reshape(count, peers * bins, view[3])

    demixed_real = apply(mix_real, real_part) - apply(mix_imag, imag_part)
    demixed_imag = apply(mix_real, imag_part) + apply(mix_imag, real_part)
    return (jnp.stack([demixed_real, demixed_imag]), variances)


def solution(mesh):
    in_specs = (P(None, None, "freq", "frame"), P(), P(), P(), P(), P(), P(), P())
    out_specs = (P(None, None, "freq", "frame"), P(None, "freq", "frame"))
    return jax.shard_map(
        on_device, mesh=mesh, in_specs=in_specs, out_specs=out_specs, check_vma=False
    )
```
